32 devices in a mesh: groups: 1, ctx: 8 (over z, y), head: 2 (over x), rep: 2 (over core).
Axes of the slice: x: 2, y: 2, z: 4, core: 2. Of those that a mesh axis runs over, the one named last changes fastest.
Arguments:
- queries: bfloat16 [16, 512, 4096], P(('groups', 'ctx'), 'rep', 'head'), may hold values from -6 to 6
- prefill_keys: bfloat16 [16, 512, 1024], P(('groups', 'ctx'), 'rep', 'head'), may hold values from -6 to 6
- prefill_values: bfloat16 [16, 512, 1024], P(('groups', 'ctx'), 'rep', 'head'), may hold values from -6 to 6
- context_keys: bfloat16 [16384, 1024], P(('groups', 'ctx'), 'head'), may hold values from -6 to 6
- context_values: bfloat16 [16384, 1024], P(('groups', 'ctx'), 'head'), may hold values from -6 to 6
- picks: int32 [16, 32, 3], P(('groups', 'ctx'), 'head'), may hold values from 0 to 47, as said below
Outputs:
- attended: bfloat16 [16, 512, 4096], P(('groups', 'ctx'), 'rep', 'head')
The draws below stay inside these ranges and needn't reach their ends.
Inputs may be any that keep to these rules, and one draw needn't show every extreme that they name: `picks`: row [b, h] is increasing; its last entry is 32 + b and its first two are cache blocks. Among the first two entries of the rows of the 2 query blocks that start at a multiple of 2 and the 16 heads of one run that starts at a multiple of 16, at most 16 lie in the 4 blocks that start at one multiple of 4, and for every such set of rows some such set of blocks holds exactly 16 of them.
All inputs are finite; a program needn't handle non-finite values.
Results may differ from the reference program's by a relative error of at most 0.0055.
Values may be sent and summed in bfloat16 or wider, within the bound.
No kernel may reach another device: no remote copies, remote signals or barrier semaphores. Data moves between devices by JAX's collectives and lax.ppermute only.
A program may use at most 64 MiB of HBM per device.

```python
import jax
import jax.numpy as jnp
from jax import lax

QUERY_HEAD_COUNT = 32
KEY_VALUE_HEADS = 8
HEAD_WIDTH = 128
BLOCK_TOKENS = 512
QB_DEV = 2
BLK_DEV = 4
CACHE_BLOCKS = 32
CACHE_TOKENS = 16384
QUERY_BLOCKS = 16
PREFILL_TOKENS = 8192
CAP = 16
N_CTX = 8
N_HEAD = 2


def key_record_field(key, salt, stack_height):
    array_shape = (stack_height, KEY_VALUE_HEADS, HEAD_WIDTH)
    record_field = jnp.clip(jax.random.normal(jax.random.fold_in(key, salt), array_shape, jnp.float32), -6.0, 6.0)
    return record_field.reshape(stack_height, KEY_VALUE_HEADS * HEAD_WIDTH).astype(jnp.bfloat16)


def draw_queries(key, part):
    array_shape = (PREFILL_TOKENS, QUERY_HEAD_COUNT, HEAD_WIDTH)
    record_field = jnp.clip(jax.random.normal(jax.random.fold_in(key, 11), array_shape, jnp.float32), -6.0, 6.0)
    return record_field.reshape(QUERY_BLOCKS, BLOCK_TOKENS, QUERY_HEAD_COUNT * HEAD_WIDTH).astype(jnp.bfloat16)


def draw_prefill_keys(key, part):
    return key_record_field(key, 21, PREFILL_TOKENS).reshape(QUERY_BLOCKS, BLOCK_TOKENS, KEY_VALUE_HEADS * HEAD_WIDTH)


def draw_context_keys(key, part):
    return key_record_field(key, 31, CACHE_TOKENS)


def draw_picks(key, part):
    head_grouping = QUERY_HEAD_COUNT // N_HEAD
    runs = QB_DEV * head_grouping
    needed = 2 * runs
    slot_total = N_CTX * CAP
    tokens = jnp.arange(slot_total)
    columns = []
    for head_index in range(N_HEAD):
        head_key = jax.random.fold_in(key, 100 + head_index)
        hottest = jax.random.randint(jax.random.fold_in(head_key, 1), (), 0, N_CTX)

        def single(row_key, row_index):
            subkeys = jax.random.split(row_key, 5)
            shuffled = jax.random.permutation(subkeys[0], slot_total)
            ranking = jnp.where(tokens // CAP == hottest, tokens % CAP, CAP + shuffled)
            taken = jnp.argsort(ranking, stable=True)[:needed]
            taken = jax.random.permutation(subkeys[1], taken)
            holders = (taken // CAP).reshape(runs, 2)
            leading = jax.random.randint(subkeys[2], (runs,), 0, BLK_DEV)
            shifted = (leading + 1 + jax.random.randint(subkeys[3], (runs,), 0, BLK_DEV - 1)) % BLK_DEV
            loose = jax.random.randint(subkeys[4], (runs,), 0, BLK_DEV)
            trailing = jnp.where(holders[:, 0] == holders[:, 1], shifted, loose)
            earlier = holders[:, 0] * BLK_DEV + leading
            later = holders[:, 1] * BLK_DEV + trailing
            ownblock = CACHE_BLOCKS + row_index * QB_DEV + jnp.arange(runs, dtype=jnp.int32) // head_grouping
            stacked = jnp.stack([jnp.minimum(earlier, later), jnp.maximum(earlier, later), ownblock], axis=1)
            return stacked.reshape(QB_DEV, head_grouping, 3)
        row_keys = jax.random.split(jax.random.fold_in(head_key, 2), N_CTX)
        columns.append(jax.vmap(single)(row_keys, jnp.arange(N_CTX, dtype=jnp.int32)))
    return jnp.concatenate(columns, axis=2).reshape(QUERY_BLOCKS, QUERY_HEAD_COUNT, 3).astype(jnp.int32)


def block_levels(stream_key, extent, cuts, smallest, largest):
    factor_of, own = 1.0, jax.random.fold_in(stream_key, 6)
    for axis_at, blocks in cuts:
        heights = jnp.exp(jax.random.uniform(jax.random.fold_in(own, axis_at), (blocks,), jnp.float32, smallest / len(cuts), largest / len(cuts)))
        factor_of = factor_of * jnp.repeat(heights, extent[axis_at] // blocks).reshape([-1 if axis == axis_at else 1 for axis in range(len(extent))])
    return factor_of


def normal_values(key, extent, scale, most, shards=(), kind=jnp.bfloat16):
    array = scale * jax.random.normal(key, extent, jnp.float32)
    if shards:
        array = array * block_levels(key, extent, shards, -0.22, 0.18)
    return jnp.clip(array, -most, most).astype(kind)


def setup_inputs(seed: int = 0, part: int = 0) -> dict:
    arg_keys = jax.random.split(jax.random.key(seed), 7)
    part_splits = jax.random.split(jax.random.fold_in(arg_keys[6], part), 7)
    return {
        "queries": draw_queries(jax.random.fold_in(jax.random.fold_in(arg_keys[6], part), 71), part),
        "prefill_keys": draw_prefill_keys(jax.random.fold_in(jax.random.fold_in(arg_keys[6], part), 71), part),
        "prefill_values": normal_values(part_splits[2], (QUERY_BLOCKS, BLOCK_TOKENS, KEY_VALUE_HEADS * HEAD_WIDTH), 1.0, 6.0, ((0, 8), (1, 2), (2, 2))),
        "context_keys": draw_context_keys(jax.random.fold_in(jax.random.fold_in(arg_keys[6], part), 71), part),
        "context_values": normal_values(part_splits[4], (CACHE_TOKENS, KEY_VALUE_HEADS * HEAD_WIDTH), 1.0, 6.0, ((0, 8), (1, 2))),
        "picks": draw_picks(jax.random.fold_in(jax.random.fold_in(arg_keys[6], part), 71), part),
    }


NEGATIVE = -1e30


def partial_attention(scores, values, allowed, pattern):
    scores = jnp.where(allowed, scores, NEGATIVE)
    highest = jnp.max(scores, axis=-1, keepdims=True)
    weights = jnp.exp(scores - highest)
    totals = jnp.sum(weights, axis=-1, keepdims=True)
    rounded = lax.optimization_barrier(weights.astype(jnp.bfloat16)).astype(jnp.float32)
    mixed = jnp.einsum(pattern, rounded, values.astype(jnp.float32))
    return mixed / totals, highest[..., 0] + jnp.log(totals[..., 0])


def reference(queries, prefill_keys, prefill_values, context_keys, context_values, picks):
    head_grouping = QUERY_HEAD_COUNT // KEY_VALUE_HEADS
    scale = HEAD_WIDTH ** -0.5
    owning_head = jnp.arange(QUERY_HEAD_COUNT, dtype=jnp.int32) // head_grouping
    key_tiles = context_keys.reshape(CACHE_BLOCKS, BLOCK_TOKENS, KEY_VALUE_HEADS, HEAD_WIDTH)
    value_tiles = context_values.reshape(CACHE_BLOCKS, BLOCK_TOKENS, KEY_VALUE_HEADS, HEAD_WIDTH)
    places = jnp.arange(BLOCK_TOKENS, dtype=jnp.int32)
    causal = places[None, :] <= places[:, None]

    def one_block(block_index):
        block_queries = lax.dynamic_index_in_dim(queries, block_index, 0, keepdims=False).reshape(BLOCK_TOKENS, QUERY_HEAD_COUNT, HEAD_WIDTH).astype(jnp.float32)
        selected_block_keys = lax.dynamic_index_in_dim(prefill_keys, block_index, 0, keepdims=False).reshape(BLOCK_TOKENS, KEY_VALUE_HEADS, HEAD_WIDTH)[:, owning_head, :].astype(jnp.float32)
        selected_block_values = lax.dynamic_index_in_dim(prefill_values, block_index, 0, keepdims=False).reshape(BLOCK_TOKENS, KEY_VALUE_HEADS, HEAD_WIDTH)[:, owning_head, :].astype(jnp.float32)
        scores = jnp.einsum("rhd,jhd->hrj", block_queries, selected_block_keys) * scale
        own_mixed, own_log = partial_attention(scores, selected_block_values, causal, "hrj,jhd->hrd")
        chosen = lax.dynamic_index_in_dim(picks, block_index, 0, keepdims=False)
        parts = [own_mixed]
        logs = [own_log]
        for column in range(2):
            blocks = chosen[:, column]
            keys_here = key_tiles[blocks, :, owning_head, :].astype(jnp.float32)
            values_here = value_tiles[blocks, :, owning_head, :].astype(jnp.float32)
            scores = jnp.einsum("rhd,hjd->hrj", block_queries, keys_here) * scale
            mixed, logged = partial_attention(scores, values_here, True, "hrj,hjd->hrd")
            mixed = lax.optimization_barrier(mixed.astype(jnp.bfloat16)).astype(jnp.float32)
            parts.append(mixed)
            logs.append(logged)
        all_logs = jnp.stack(logs, 0)
        all_mixed = jnp.stack(parts, 0)
        peak = jnp.max(all_logs, axis=0, keepdims=True)
        shares = jnp.exp(all_logs - peak)
        merged = jnp.sum(shares[..., None] * all_mixed, axis=0) / jnp.sum(shares, axis=0)[..., None]
        return jnp.transpose(merged, (1, 0, 2)).reshape(BLOCK_TOKENS, QUERY_HEAD_COUNT * HEAD_WIDTH).astype(jnp.bfloat16)

    return lax.map(one_block, jnp.arange(QUERY_BLOCKS, dtype=jnp.int32))
```

```python
import functools

import jax
import jax.numpy as jnp
from jax import lax
from jax.experimental import pallas as pl
from jax.experimental.pallas import tpu as pltpu
from jax.sharding import PartitionSpec as P

HEAD_WIDTH = 128
BLOCK_TOKENS = 512
SCALE = HEAD_WIDTH ** (-0.5)
LOG2E = 1.4426950408889634
NEGATIVE = -1e30


def scores_by_key(keys, queries):
    return lax.dot_general(
        keys, queries, (((1,), (1,)), ((), ())), preferred_element_type=jnp.float32
    )


def mix_by_width(values, weights):
    return lax.dot_general(
        values,
        weights.astype(jnp.bfloat16),
        (((0,), (0,)), ((), ())),
        preferred_element_type=jnp.float32,
    )


def own_kernel(q_ref, k_ref, v_ref, part_ref, log_ref, picked_ref, picked_log_ref):
    half = q_ref.shape[1] // 2
    visible = lax.broadcasted_iota(jnp.int32, (half, half), 0) <= lax.broadcasted_iota(
        jnp.int32, (half, half), 1
    )
    early_keys, late_keys = k_ref[0, :half], k_ref[0, half:]
    early_queries, late_queries = q_ref[0, :half], q_ref[0, half:]

    first = jnp.where(visible, scores_by_key(early_keys, early_queries), NEGATIVE)
    highest = jnp.max(first, axis=0, keepdims=True)
    weights = jnp.exp2((first - highest) * (SCALE * LOG2E))
    total = jnp.sum(weights, axis=0, keepdims=True)
    part_ref[0, :, :half] = mix_by_width(v_ref[0, :half], weights) / total
    log_ref[0, :, :half] = highest * SCALE + jnp.log(total)

    before = scores_by_key(early_keys, late_queries)
    within = jnp.where(visible, scores_by_key(late_keys, late_queries), NEGATIVE)
    highest = jnp.maximum(
        jnp.max(before, axis=0, keepdims=True), jnp.max(within, axis=0, keepdims=True)
    )
    before = jnp.exp2((before - highest) * (SCALE * LOG2E))
    within = jnp.exp2((within - highest) * (SCALE * LOG2E))
    total = jnp.sum(before, axis=0, keepdims=True) + jnp.sum(within, axis=0, keepdims=True)
    mixed = mix_by_width(v_ref[0, :half], before) + mix_by_width(v_ref[0, half:], within)
    part_ref[0, :, half:] = mixed / total
    log_ref[0, :, half:] = highest * SCALE + jnp.log(total)


def own_attention(queries, keys, values, head_grouping):
    blocks, rows, width = queries.shape
    heads = width // HEAD_WIDTH
    count = blocks * heads
    items = 2 * count
    query_spec = pl.BlockSpec((1, rows, HEAD_WIDTH), lambda n: (lax.div(n, heads), 0, lax.rem(n, heads)))
    key_spec = pl.BlockSpec(
        (1, rows, HEAD_WIDTH), lambda n: (lax.div(n, heads), 0, lax.div(lax.rem(n, heads), head_grouping))
    )
    return pl.pallas_call(
        own_kernel,
        grid=(count,),
        in_specs=[query_spec, key_spec, key_spec],
        out_specs=[
            pl.BlockSpec((1, HEAD_WIDTH, rows), lambda n: (n, 0, 0)),
            pl.BlockSpec((1, 1, rows), lambda n: (n, 0, 0)),
            pl.BlockSpec(memory_space=pl.ANY),
            pl.BlockSpec(memory_space=pl.ANY),
        ],
        out_shape=[
            jax.ShapeDtypeStruct((count, HEAD_WIDTH, rows), jnp.float32),
            jax.ShapeDtypeStruct((count, 1, rows), jnp.float32),
            jax.ShapeDtypeStruct((items + 2, HEAD_WIDTH, rows), jnp.bfloat16),
            jax.ShapeDtypeStruct((items + 2, 1, rows), jnp.float32),
        ],
        cost_estimate=pl.CostEstimate(
            flops=count * rows * rows * HEAD_WIDTH * 4,
            transcendentals=count * rows * rows,
            bytes_accessed=count * rows * HEAD_WIDTH * 8,
        ),
        name="own_attention",
    )(queries, keys, values)


def pick_kernel(table, count, q_hbm, k_hbm, v_hbm, part_in, log_in, part_hbm, log_hbm):
    rows = q_hbm.shape[1]

    def attend(q_ref, k_ref, v_ref, part_ref, log_ref):
        scores = scores_by_key(k_ref[...], q_ref[0])
        highest = jnp.max(scores, axis=0, keepdims=True)
        weights = jnp.exp2((scores - highest) * (SCALE * LOG2E))
        total = jnp.sum(weights, axis=0, keepdims=True)
        part_ref[0] = (mix_by_width(v_ref[...], weights) / total).astype(part_ref.dtype)
        log_ref[0] = highest * SCALE + jnp.log(total)

    tile = pl.BlockSpec((BLOCK_TOKENS, HEAD_WIDTH), lambda n: (table[1, n], table[2, n]))
    pltpu.emit_pipeline(
        attend,
        grid=(count[0],),
        in_specs=[
            pl.BlockSpec((1, rows, HEAD_WIDTH), lambda n: (table[3, n], 0, table[4, n])),
            tile,
            tile,
        ],
        out_specs=[
            pl.BlockSpec((1, HEAD_WIDTH, rows), lambda n: (table[0, n], 0, 0)),
            pl.BlockSpec((1, 1, rows), lambda n: (table[0, n], 0, 0)),
        ],
    )(q_hbm, k_hbm, v_hbm, part_hbm, log_hbm)


def pick_attention(table, count, queries, keys, values, parts, logs):
    blocks, rows, width = queries.shape
    expected = 2 * blocks * (width // HEAD_WIDTH) // 8
    smem = pl.BlockSpec(memory_space=pltpu.SMEM)
    anywhere = pl.BlockSpec(memory_space=pl.ANY)
    return pl.pallas_call(
        pick_kernel,
        in_specs=[smem, smem] + [anywhere] * 5,
        out_specs=[anywhere, anywhere],
        out_shape=[
            jax.ShapeDtypeStruct(parts.shape, parts.dtype),
            jax.ShapeDtypeStruct(logs.shape, logs.dtype),
        ],
        input_output_aliases={5: 0, 6: 1},
        cost_estimate=pl.CostEstimate(
            flops=expected * rows * BLOCK_TOKENS * HEAD_WIDTH * 4,
            transcendentals=expected * rows * BLOCK_TOKENS,
            bytes_accessed=expected * rows * HEAD_WIDTH * 8,
        ),
        name="pick_attention",
    )(table, count.reshape(1), queries, keys, values, parts, logs)


def merge_kernel(rep, own_ref, own_log_ref, part_ref, log_ref, keep_ref, send_ref):
    half = keep_ref.shape[1]
    own_log, first_log, second_log = own_log_ref[0], log_ref[0], log_ref[1]
    top = jnp.maximum(own_log, jnp.maximum(first_log, second_log))
    own_share = jnp.exp(own_log - top)
    first_share = jnp.exp(first_log - top)
    second_share = jnp.exp(second_log - top)
    merged = (
        own_share * own_ref[0]
        + first_share * part_ref[0].astype(jnp.float32)
        + second_share * part_ref[1].astype(jnp.float32)
    ) / (own_share + first_share + second_share)
    early = merged[:, :half].T.astype(keep_ref.dtype)
    late = merged[:, half:].T.astype(keep_ref.dtype)
    keep_ref[0] = jnp.where(rep[0] == 0, early, late)
    send_ref[0] = jnp.where(rep[0] == 0, late, early)


def merge(rep, own, own_log, parts, logs, blocks, full_width):
    count, _, rows = own.shape
    heads = count // blocks
    half = rows // 2
    return pl.pallas_call(
        merge_kernel,
        grid_spec=pltpu.PrefetchScalarGridSpec(
            num_scalar_prefetch=1,
            grid=(count,),
            in_specs=[
                pl.BlockSpec((1, HEAD_WIDTH, rows), lambda n, r: (n, 0, 0)),
                pl.BlockSpec((1, 1, rows), lambda n, r: (n, 0, 0)),
                pl.BlockSpec((2, HEAD_WIDTH, rows), lambda n, r: (n, 0, 0)),
                pl.BlockSpec((2, 1, rows), lambda n, r: (n, 0, 0)),
            ],
            out_specs=[
                pl.BlockSpec(
                    (1, half, HEAD_WIDTH),
                    lambda n, r: (lax.div(n, heads), 0, r[0] * heads + lax.rem(n, heads)),
                ),
                pl.BlockSpec((1, half, HEAD_WIDTH), lambda n, r: (lax.div(n, heads), 0, lax.rem(n, heads))),
            ],
        ),
        out_shape=[
            jax.ShapeDtypeStruct((blocks, half, full_width), jnp.bfloat16),
            jax.ShapeDtypeStruct((blocks, half, heads * HEAD_WIDTH), jnp.bfloat16),
        ],
        cost_estimate=pl.CostEstimate(
            flops=count * rows * HEAD_WIDTH * 8,
            transcendentals=count * rows * 3,
            bytes_accessed=count * rows * HEAD_WIDTH * 10,
        ),
        name="merge_parts",
    )(rep, own, own_log, parts, logs)


def ring_order(count):
    return list(range(0, count, 2)) + list(range(count - 1, 0, -2))


def item_tables(holders, tiles, key_heads, blocks, heads, wanted, items):
    mine = holders[None, :] == wanted[:, None]
    place = jnp.cumsum(mine.astype(jnp.int32), axis=1) - 1
    slot = jnp.arange(items)
    chosen = mine[:, :, None] & (place[:, :, None] == slot[None, None, :])
    columns = jnp.stack([jnp.arange(items), tiles, key_heads, blocks, heads])
    filled = jnp.sum(jnp.where(chosen[:, None], columns[None, :, :, None], 0), axis=2)
    counts = jnp.sum(mine.astype(jnp.int32), axis=1)
    spare = (slot[None, :] >= counts[:, None])[:, None, :] & (jnp.arange(5) == 0)[None, :, None]
    return jnp.where(spare, items, filled), jnp.maximum(counts, 1)


def body(queries, prefill_keys, prefill_values, context_keys, context_values, picks):
    local_count, stack_height, full_width = queries.shape
    rep_size = lax.axis_size("rep")
    ctx_size = lax.axis_size("ctx")
    rep_index = lax.axis_index("rep")
    ctx_index = lax.axis_index("ctx")
    width = full_width // rep_size
    key_width = prefill_keys.shape[2] // rep_size
    heads = width // HEAD_WIDTH
    head_grouping = width // key_width
    blocks_here = context_keys.shape[0] // BLOCK_TOKENS
    items = 2 * local_count * heads
    swap = [(0, 1), (1, 0)]

    def columns_of(value, which, size):
        return lax.dynamic_slice_in_dim(value, which * size, size, axis=value.ndim - 1)

    own_shard = (
        columns_of(context_keys, rep_index, key_width),
        columns_of(context_values, rep_index, key_width),
    )
    order = ring_order(ctx_size)
    onward = [(order[n], order[(n + 1) % ctx_size]) for n in range(ctx_size)]
    backward = [(target, source) for source, target in onward]
    shards = {0: own_shard}
    ahead, behind = own_shard, own_shard
    for step in range(1, (ctx_size - 1) // 2 + 1):
        ahead = tuple(lax.ppermute(part, "ctx", onward) for part in ahead)
        behind = tuple(lax.ppermute(part, "ctx", backward) for part in behind)
        shards[-step], shards[step] = ahead, behind
    if ctx_size % 2 == 0:
        shards[ctx_size // 2] = (
            lax.ppermute(ahead[0], "ctx", onward),
            lax.ppermute(behind[1], "ctx", backward),
        )

    other = rep_size - 1 - rep_index

    def all_rows(value, size):
        kept = columns_of(value, rep_index, size)
        came = lax.ppermute(columns_of(value, other, size), "rep", swap)
        return jnp.where(
            rep_index == 0,
            jnp.concatenate([kept, came], axis=1),
            jnp.concatenate([came, kept], axis=1),
        )

    block_queries = all_rows(queries, width)
    block_keys = all_rows(prefill_keys, key_width)
    block_values = all_rows(prefill_values, key_width)

    position_of = [0] * ctx_size
    for position, device in enumerate(order):
        position_of[device] = position
    here = jnp.array(position_of, jnp.int32)[ctx_index]
    distances = sorted(shards, key=abs)
    wanted = jnp.array(order, jnp.int32)[(here + jnp.array(distances, jnp.int32)) % ctx_size]
    mine = lax.dynamic_slice_in_dim(picks[:, :, :2], rep_index * heads, heads, axis=1).reshape(-1)
    place = jnp.arange(items)
    head = place // 2 % heads
    holders = mine // blocks_here
    tables, counts = item_tables(
        holders,
        mine - holders * blocks_here,
        head // head_grouping,
        place // (2 * heads),
        head,
        wanted,
        items,
    )

    own, own_log, parts, logs = own_attention(
        block_queries, block_keys, block_values, head_grouping
    )
    for n, distance in enumerate(distances):
        keys, values = shards[distance]
        parts, logs = pick_attention(
            tables[n], counts[n], block_queries, keys, values, parts, logs
        )
    result, leaving = merge(
        rep_index.reshape(1), own, own_log, parts, logs, local_count, full_width
    )
    arriving = lax.ppermute(leaving, "rep", swap)
    return lax.dynamic_update_slice_in_dim(result, arriving, other * width, axis=2)


def solution(mesh):
    return jax.shard_map(
        body,
        mesh=mesh,
        in_specs=(
            P(("groups", "ctx"), "rep", "head"),
            P(("groups", "ctx"), "rep", "head"),
            P(("groups", "ctx"), "rep", "head"),
            P(("groups", "ctx"), "head"),
            P(("groups", "ctx"), "head"),
            P(("groups", "ctx"), "head", None),
        ),
        out_specs=P(("groups", "ctx"), "rep", "head"),
        check_vma=False,
    )
```

```python
import jax
import jax.numpy as jnp
from jax import lax
from jax.experimental import pallas as pl
from jax.experimental.pallas import tpu as pltpu
from jax.sharding import PartitionSpec as P


HEAD_WIDTH = 128
BLOCK_TOKENS = 512
SCALE = HEAD_WIDTH ** (-0.5)
LOG2E = 1.4426950408889634
NEGATIVE = -1e30


def scores_by_key(keys, queries):
    return lax.dot_general(
        keys, queries, (((1,), (1,)), ((), ())), preferred_element_type=jnp.float32
    )


def mix_by_width(values, weights):
    return lax.dot_general(
        values,
        weights.astype(jnp.bfloat16),
        (((0,), (0,)), ((), ())),
        preferred_element_type=jnp.float32,
    )


def own_kernel(q_ref, k_ref, v_ref, part_ref, log_ref, *unwritten):
    half = q_ref.shape[1] // 2
    visible = lax.broadcasted_iota(jnp.int32, (half, half), 0) <= lax.broadcasted_iota(
        jnp.int32, (half, half), 1
    )
    early_keys, late_keys = k_ref[0, :half], k_ref[0, half:]
    early_queries, late_queries = q_ref[0, :half], q_ref[0, half:]

    first = jnp.where(visible, scores_by_key(early_keys, early_queries), NEGATIVE)
    highest = jnp.max(first, axis=0, keepdims=True)
    weights = jnp.exp2((first - highest) * (SCALE * LOG2E))
    total = jnp.sum(weights, axis=0, keepdims=True)
    part_ref[0, :, :half] = mix_by_width(v_ref[0, :half], weights) / total
    log_ref[0, :, :half] = highest * SCALE + jnp.log(total)

    before = scores_by_key(early_keys, late_queries)
    within = jnp.where(visible, scores_by_key(late_keys, late_queries), NEGATIVE)
    highest = jnp.maximum(
        jnp.max(before, axis=0, keepdims=True), jnp.max(within, axis=0, keepdims=True)
    )
    before = jnp.exp2((before - highest) * (SCALE * LOG2E))
    within = jnp.exp2((within - highest) * (SCALE * LOG2E))
    total = jnp.sum(before, axis=0, keepdims=True) + jnp.sum(within, axis=0, keepdims=True)
    mixed = mix_by_width(v_ref[0, :half], before) + mix_by_width(v_ref[0, half:], within)
    part_ref[0, :, half:] = mixed / total
    log_ref[0, :, half:] = highest * SCALE + jnp.log(total)


def own_attention(queries, keys, values, head_grouping, full_width):
    blocks, rows, width = queries.shape
    heads = width // HEAD_WIDTH
    count = blocks * heads
    items = 2 * count
    query_spec = pl.BlockSpec((1, rows, HEAD_WIDTH), lambda n: (lax.div(n, heads), 0, lax.rem(n, heads)))
    key_spec = pl.BlockSpec(
        (1, rows, HEAD_WIDTH), lambda n: (lax.div(n, heads), 0, lax.div(lax.rem(n, heads), head_grouping))
    )
    return pl.pallas_call(
        own_kernel,
        grid=(count,),
        in_specs=[query_spec, key_spec, key_spec],
        out_specs=[
            pl.BlockSpec((1, HEAD_WIDTH, rows), lambda n: (n, 0, 0)),
            pl.BlockSpec((1, 1, rows), lambda n: (n, 0, 0)),
        ]
        + [pl.BlockSpec(memory_space=pl.ANY)] * 4,
        out_shape=[
            jax.ShapeDtypeStruct((count, HEAD_WIDTH, rows), jnp.float32),
            jax.ShapeDtypeStruct((count, 1, rows), jnp.float32),
            jax.ShapeDtypeStruct((items + 2, HEAD_WIDTH, rows), jnp.bfloat16),
            jax.ShapeDtypeStruct((items + 2, 1, rows), jnp.float32),
            jax.ShapeDtypeStruct((blocks, rows // 2, full_width), jnp.bfloat16),
            jax.ShapeDtypeStruct((blocks, rows // 2, width), jnp.bfloat16),
        ],
        cost_estimate=pl.CostEstimate(
            flops=count * rows * rows * HEAD_WIDTH * 4,
            transcendentals=count * rows * rows,
            bytes_accessed=count * rows * HEAD_WIDTH * 8,
        ),
        name="own_attention",
    )(queries, keys, values)


def pick_kernel(table, count, q_hbm, k_hbm, v_hbm, part_in, log_in, part_hbm, log_hbm):
    rows = q_hbm.shape[1]

    def attend(q_ref, k_ref, v_ref, part_ref, log_ref):
        scores = scores_by_key(k_ref[...], q_ref[0])
        highest = jnp.max(scores, axis=0, keepdims=True)
        weights = jnp.exp2((scores - highest) * (SCALE * LOG2E))
        total = jnp.sum(weights, axis=0, keepdims=True)
        part_ref[0] = (mix_by_width(v_ref[...], weights) / total).astype(part_ref.dtype)
        log_ref[0] = highest * SCALE + jnp.log(total)

    tile = pl.BlockSpec((BLOCK_TOKENS, HEAD_WIDTH), lambda n: (table[1, n], table[2, n]))
    pltpu.emit_pipeline(
        attend,
        grid=(count[0],),
        in_specs=[
            pl.BlockSpec((1, rows, HEAD_WIDTH), lambda n: (table[3, n], 0, table[4, n])),
            tile,
            tile,
        ],
        out_specs=[
            pl.BlockSpec((1, HEAD_WIDTH, rows), lambda n: (table[0, n], 0, 0)),
            pl.BlockSpec((1, 1, rows), lambda n: (table[0, n], 0, 0)),
        ],
    )(q_hbm, k_hbm, v_hbm, part_hbm, log_hbm)


def pick_attention(table, count, queries, keys, values, parts, logs):
    blocks, rows, width = queries.shape
    expected = 2 * blocks * (width // HEAD_WIDTH) // 8
    smem = pl.BlockSpec(memory_space=pltpu.SMEM)
    anywhere = pl.BlockSpec(memory_space=pl.ANY)
    return pl.pallas_call(
        pick_kernel,
        in_specs=[smem, smem] + [anywhere] * 5,
        out_specs=[anywhere, anywhere],
        out_shape=[
            jax.ShapeDtypeStruct(parts.shape, parts.dtype),
            jax.ShapeDtypeStruct(logs.shape, logs.dtype),
        ],
        input_output_aliases={5: 0, 6: 1},
        cost_estimate=pl.CostEstimate(
            flops=expected * rows * BLOCK_TOKENS * HEAD_WIDTH * 4,
            transcendentals=expected * rows * BLOCK_TOKENS,
            bytes_accessed=expected * rows * HEAD_WIDTH * 8,
        ),
        name="pick_attention",
    )(table, count.reshape(1), queries, keys, values, parts, logs)


def merge_kernel(
    rep, ready, count, own_hbm, own_log_hbm, part_hbm, log_hbm, keep_in, send_in, keep_hbm, send_hbm
):
    rows = own_hbm.shape[2]
    half = rows // 2
    heads = send_hbm.shape[2] // HEAD_WIDTH

    def combine(own_ref, own_log_ref, part_ref, log_ref, keep_ref, send_ref):
        own_log, first_log, second_log = own_log_ref[0], log_ref[0], log_ref[1]
        top = jnp.maximum(own_log, jnp.maximum(first_log, second_log))
        own_share = jnp.exp(own_log - top)
        first_share = jnp.exp(first_log - top)
        second_share = jnp.exp(second_log - top)
        merged = (
            own_share * own_ref[0]
            + first_share * part_ref[0].astype(jnp.float32)
            + second_share * part_ref[1].astype(jnp.float32)
        ) / (own_share + first_share + second_share)
        early = merged[:, :half].T.astype(keep_ref.dtype)
        late = merged[:, half:].T.astype(keep_ref.dtype)
        keep_ref[0] = jnp.where(rep[0] == 0, early, late)
        send_ref[0] = jnp.where(rep[0] == 0, late, early)

    def place(n):
        return lax.div(ready[n], heads), lax.rem(ready[n], heads)

    pltpu.emit_pipeline(
        combine,
        grid=(count[0],),
        in_specs=[
            pl.BlockSpec((1, HEAD_WIDTH, rows), lambda n: (ready[n], 0, 0)),
            pl.BlockSpec((1, 1, rows), lambda n: (ready[n], 0, 0)),
            pl.BlockSpec((2, HEAD_WIDTH, rows), lambda n: (ready[n], 0, 0)),
            pl.BlockSpec((2, 1, rows), lambda n: (ready[n], 0, 0)),
        ],
        out_specs=[
            pl.BlockSpec(
                (1, half, HEAD_WIDTH), lambda n: (place(n)[0], 0, rep[0] * heads + place(n)[1])
            ),
            pl.BlockSpec((1, half, HEAD_WIDTH), lambda n: (place(n)[0], 0, place(n)[1])),
        ],
    )(own_hbm, own_log_hbm, part_hbm, log_hbm, keep_hbm, send_hbm)


def merge(rep, ready, count, own, own_log, parts, logs, keep, send):
    heads, _, rows = own.shape
    smem = pl.BlockSpec(memory_space=pltpu.SMEM)
    anywhere = pl.BlockSpec(memory_space=pl.ANY)
    return pl.pallas_call(
        merge_kernel,
        in_specs=[smem] * 3 + [anywhere] * 6,
        out_specs=[anywhere, anywhere],
        out_shape=[
            jax.ShapeDtypeStruct(keep.shape, keep.dtype),
            jax.ShapeDtypeStruct(send.shape, send.dtype),
        ],
        input_output_aliases={7: 0, 8: 1},
        cost_estimate=pl.CostEstimate(
            flops=heads * rows * HEAD_WIDTH * 8,
            transcendentals=heads * rows * 3,
            bytes_accessed=heads * rows * HEAD_WIDTH * 10,
        ),
        name="merge_parts",
    )(rep.reshape(1), ready, count.reshape(1), own, own_log, parts, logs, keep, send)


def ring_order(count):
    return list(range(0, count, 2)) + list(range(count - 1, 0, -2))


def compacted(mask, columns, spare):
    place = jnp.cumsum(mask.astype(jnp.int32), axis=1) - 1
    slot = jnp.arange(mask.shape[1])
    chosen = mask[:, :, None] & (place[:, :, None] == slot[None, None, :])
    filled = jnp.sum(jnp.where(chosen[:, None], columns[None, :, :, None], 0), axis=2)
    counts = jnp.sum(mask.astype(jnp.int32), axis=1)
    empty = (slot[None, :] >= counts[:, None])[:, None, :]
    return jnp.where(empty, spare[None, :, None], filled), counts


def body(queries, prefill_keys, prefill_values, context_keys, context_values, picks):
    local_count, _, full_width = queries.shape
    rep_size = lax.axis_size("rep")
    ctx_size = lax.axis_size("ctx")
    rep_index = lax.axis_index("rep")
    ctx_index = lax.axis_index("ctx")
    width = full_width // rep_size
    key_width = prefill_keys.shape[2] // rep_size
    heads = width // HEAD_WIDTH
    head_grouping = width // key_width
    blocks_here = context_keys.shape[0] // BLOCK_TOKENS
    items = 2 * local_count * heads
    swap = [(0, 1), (1, 0)]

    def columns_of(value, which, size):
        return lax.dynamic_slice_in_dim(value, which * size, size, axis=value.ndim - 1)

    own_shard = (
        columns_of(context_keys, rep_index, key_width),
        columns_of(context_values, rep_index, key_width),
    )
    order = ring_order(ctx_size)
    onward = [(order[n], order[(n + 1) % ctx_size]) for n in range(ctx_size)]
    backward = [(target, source) for source, target in onward]

    def hop(value, pairs):
        return lax.ppermute(value, "ctx", pairs)

    shards = {0: own_shard}
    ahead, behind = own_shard, own_shard
    full_steps = (ctx_size - 1) // 2
    for step in range(1, full_steps + 1):
        ahead = (hop(ahead[0], onward), hop(ahead[1], onward))
        behind = (hop(behind[0], backward), hop(behind[1], backward))
        shards[-step], shards[step] = ahead, behind
    if ctx_size % 2 == 0:
        step = full_steps + 1
        shards[step] = (hop(ahead[0], onward), hop(behind[1], backward))

    other = rep_size - 1 - rep_index

    def all_rows(value, size):
        kept = columns_of(value, rep_index, size)
        came = lax.ppermute(columns_of(value, other, size), "rep", swap)
        return jnp.where(
            rep_index == 0,
            jnp.concatenate([kept, came], axis=1),
            jnp.concatenate([came, kept], axis=1),
        )

    block_queries = all_rows(queries, width)
    block_keys = all_rows(prefill_keys, key_width)
    block_values = all_rows(prefill_values, key_width)

    position_of = [0] * ctx_size
    for position, device in enumerate(order):
        position_of[device] = position
    here = jnp.array(position_of, jnp.int32)[ctx_index]
    distances = sorted(shards, key=abs)
    wanted = jnp.array(order, jnp.int32)[(here + jnp.array(distances, jnp.int32)) % ctx_size]
    mine = lax.dynamic_slice_in_dim(picks[:, :, :2], rep_index * heads, heads, axis=1).reshape(-1)
    place = jnp.arange(items)
    head = place // 2 % heads
    holders = mine // blocks_here
    columns = jnp.stack(
        [
            place,
            mine - holders * blocks_here,
            head // head_grouping,
            place // (2 * heads),
            head,
        ]
    )
    spare = jnp.array([items, 0, 0, 0, 0], jnp.int32)
    tables, counts = compacted(holders[None, :] == wanted[:, None], columns, spare)
    counts = jnp.maximum(counts, 1)
    waiting = jnp.any(holders.reshape(-1, 2) == wanted[-1], axis=1)
    ready, ready_counts = compacted(
        jnp.stack([~waiting, waiting]),
        jnp.arange(items // 2)[None],
        jnp.zeros((1,), jnp.int32),
    )
    ready_counts = jnp.maximum(ready_counts, 1)

    own, own_log, parts, logs, keep, send = own_attention(
        block_queries, block_keys, block_values, head_grouping, full_width
    )
    for n, distance in enumerate(distances):
        keys, values = shards[distance]
        if n == len(distances) - 1:
            keep, send = merge(
                rep_index, ready[0, 0], ready_counts[0], own, own_log, parts, logs, keep, send
            )
        parts, logs = pick_attention(tables[n], counts[n], block_queries, keys, values, parts, logs)
    keep, send = merge(
        rep_index, ready[1, 0], ready_counts[1], own, own_log, parts, logs, keep, send
    )
    arriving = lax.ppermute(send, "rep", swap)
    return lax.dynamic_update_slice_in_dim(keep, arriving, other * width, axis=2)


def solution(mesh):
    return jax.shard_map(
        body,
        mesh=mesh,
        in_specs=(
            P(("groups", "ctx"), "rep", "head"),
            P(("groups", "ctx"), "rep", "head"),
            P(("groups", "ctx"), "rep", "head"),
            P(("groups", "ctx"), "head"),
            P(("groups", "ctx"), "head"),
            P(("groups", "ctx"), "head", None),
        ),
        out_specs=P(("groups", "ctx"), "rep", "head"),
        check_vma=False,
    )
```

```python
import jax
import jax.numpy as jnp
from jax import lax
from jax.experimental import pallas as pl
from jax.experimental.pallas import tpu as pltpu
from jax.sharding import PartitionSpec as P


HEAD_WIDTH = 128
BLOCK_TOKENS = 512
SCALE = HEAD_WIDTH ** (-0.5)
LOG2E = 1.4426950408889634
NEGATIVE = -1e30
PIECES = 2


def scores_by_key(keys, queries):
    return lax.dot_general(
        keys, queries, (((1,), (1,)), ((), ())), preferred_element_type=jnp.float32
    )


def mix_by_width(values, weights):
    return lax.dot_general(
        values,
        weights.astype(jnp.bfloat16),
        (((0,), (0,)), ((), ())),
        preferred_element_type=jnp.float32,
    )


def own_kernel(q_ref, k_ref, v_ref, part_ref, log_ref, *unwritten):
    half = q_ref.shape[1] // 2
    visible = lax.broadcasted_iota(jnp.int32, (half, half), 0) <= lax.broadcasted_iota(
        jnp.int32, (half, half), 1
    )
    early_keys, late_keys = k_ref[0, :half], k_ref[0, half:]
    early_queries, late_queries = q_ref[0, :half], q_ref[0, half:]

    first = jnp.where(visible, scores_by_key(early_keys, early_queries), NEGATIVE)
    highest = jnp.max(first, axis=0, keepdims=True)
    weights = jnp.exp2((first - highest) * (SCALE * LOG2E))
    total = jnp.sum(weights, axis=0, keepdims=True)
    part_ref[0, :, :half] = mix_by_width(v_ref[0, :half], weights) / total
    log_ref[0, :, :half] = highest * SCALE + jnp.log(total)

    before = scores_by_key(early_keys, late_queries)
    within = jnp.where(visible, scores_by_key(late_keys, late_queries), NEGATIVE)
    highest = jnp.maximum(
        jnp.max(before, axis=0, keepdims=True), jnp.max(within, axis=0, keepdims=True)
    )
    before = jnp.exp2((before - highest) * (SCALE * LOG2E))
    within = jnp.exp2((within - highest) * (SCALE * LOG2E))
    total = jnp.sum(before, axis=0, keepdims=True) + jnp.sum(within, axis=0, keepdims=True)
    mixed = mix_by_width(v_ref[0, :half], before) + mix_by_width(v_ref[0, half:], within)
    part_ref[0, :, half:] = mixed / total
    log_ref[0, :, half:] = highest * SCALE + jnp.log(total)


def own_attention(queries, keys, values, head_grouping, full_width):
    blocks, rows, width = queries.shape
    heads = width // HEAD_WIDTH
    count = blocks * heads
    items = 2 * count
    query_spec = pl.BlockSpec((1, rows, HEAD_WIDTH), lambda n: (lax.div(n, heads), 0, lax.rem(n, heads)))
    key_spec = pl.BlockSpec(
        (1, rows, HEAD_WIDTH), lambda n: (lax.div(n, heads), 0, lax.div(lax.rem(n, heads), head_grouping))
    )
    return pl.pallas_call(
        own_kernel,
        grid=(count,),
        in_specs=[query_spec, key_spec, key_spec],
        out_specs=[
            pl.BlockSpec((1, HEAD_WIDTH, rows), lambda n: (n, 0, 0)),
            pl.BlockSpec((1, 1, rows), lambda n: (n, 0, 0)),
        ]
        + [pl.BlockSpec(memory_space=pl.ANY)] * 4,
        out_shape=[
            jax.ShapeDtypeStruct((count, HEAD_WIDTH, rows), jnp.float32),
            jax.ShapeDtypeStruct((count, 1, rows), jnp.float32),
            jax.ShapeDtypeStruct((items + 2, HEAD_WIDTH, rows), jnp.bfloat16),
            jax.ShapeDtypeStruct((items + 2, 1, rows), jnp.float32),
            jax.ShapeDtypeStruct((blocks, rows // 2, full_width), jnp.bfloat16),
            jax.ShapeDtypeStruct((blocks, rows // 2, width), jnp.bfloat16),
        ],
        cost_estimate=pl.CostEstimate(
            flops=count * rows * rows * HEAD_WIDTH * 4,
            transcendentals=count * rows * rows,
            bytes_accessed=count * rows * HEAD_WIDTH * 8,
        ),
        name="own_attention",
    )(queries, keys, values)


def attend_tile(queries, keys, values):
    scores = scores_by_key(keys, queries)
    highest = jnp.max(scores, axis=0, keepdims=True)
    weights = jnp.exp2((scores - highest) * (SCALE * LOG2E))
    total = jnp.sum(weights, axis=0, keepdims=True)
    part = (mix_by_width(values, weights) / total).astype(jnp.bfloat16)
    return part, highest * SCALE + jnp.log(total)


def when_any(count, pipeline, *arrays):
    @pl.when(count > 0)
    def _():
        pipeline(*arrays)


def pick_kernel(table, count, q_hbm, k_hbm, v_hbm, part_in, log_in, part_hbm, log_hbm):
    rows = q_hbm.shape[1]

    def attend(q_ref, k_ref, v_ref, part_ref, log_ref):
        part_ref[0], log_ref[0] = attend_tile(q_ref[0], k_ref[...], v_ref[...])

    tile = pl.BlockSpec((BLOCK_TOKENS, HEAD_WIDTH), lambda n: (table[1, n], table[2, n]))
    pipeline = pltpu.emit_pipeline(
        attend,
        grid=(count[0],),
        in_specs=[
            pl.BlockSpec((1, rows, HEAD_WIDTH), lambda n: (table[3, n], 0, table[4, n])),
            tile,
            tile,
        ],
        out_specs=[
            pl.BlockSpec((1, HEAD_WIDTH, rows), lambda n: (table[0, n], 0, 0)),
            pl.BlockSpec((1, 1, rows), lambda n: (table[0, n], 0, 0)),
        ],
    )
    when_any(count[0], pipeline, q_hbm, k_hbm, v_hbm, part_hbm, log_hbm)


def pick_attention(table, count, queries, keys, values, parts, logs):
    blocks, rows, width = queries.shape
    expected = 2 * blocks * (width // HEAD_WIDTH) // 8
    smem = pl.BlockSpec(memory_space=pltpu.SMEM)
    anywhere = pl.BlockSpec(memory_space=pl.ANY)
    return pl.pallas_call(
        pick_kernel,
        in_specs=[smem, smem] + [anywhere] * 5,
        out_specs=[anywhere, anywhere],
        out_shape=[
            jax.ShapeDtypeStruct(parts.shape, parts.dtype),
            jax.ShapeDtypeStruct(logs.shape, logs.dtype),
        ],
        input_output_aliases={5: 0, 6: 1},
        cost_estimate=pl.CostEstimate(
            flops=expected * rows * BLOCK_TOKENS * HEAD_WIDTH * 4,
            transcendentals=expected * rows * BLOCK_TOKENS,
            bytes_accessed=expected * rows * HEAD_WIDTH * 8,
        ),
        name="pick_attention",
    )(table, count.reshape(1), queries, keys, values, parts, logs)


def merged_rows(rep, own, own_log, first, first_log, second, second_log):
    half = own.shape[1] // 2
    top = jnp.maximum(own_log, jnp.maximum(first_log, second_log))
    own_share = jnp.exp(own_log - top)
    first_share = jnp.exp(first_log - top)
    second_share = jnp.exp(second_log - top)
    merged = (
        own_share * own
        + first_share * first.astype(jnp.float32)
        + second_share * second.astype(jnp.float32)
    ) / (own_share + first_share + second_share)
    early = merged[:, :half].T.astype(jnp.bfloat16)
    late = merged[:, half:].T.astype(jnp.bfloat16)
    return jnp.where(rep == 0, early, late), jnp.where(rep == 0, late, early)


def merge_kernel(
    rep, ready, count, own_hbm, own_log_hbm, part_hbm, log_hbm, keep_in, send_in, keep_hbm, send_hbm
):
    rows = own_hbm.shape[2]
    half = rows // 2
    heads = send_hbm.shape[2] // HEAD_WIDTH

    def combine(own_ref, own_log_ref, part_ref, log_ref, keep_ref, send_ref):
        keep_ref[0], send_ref[0] = merged_rows(
            rep[0], own_ref[0], own_log_ref[0], part_ref[0], log_ref[0], part_ref[1], log_ref[1]
        )

    def place(n):
        return lax.div(ready[n], heads), lax.rem(ready[n], heads)

    pipeline = pltpu.emit_pipeline(
        combine,
        grid=(count[0],),
        in_specs=[
            pl.BlockSpec((1, HEAD_WIDTH, rows), lambda n: (ready[n], 0, 0)),
            pl.BlockSpec((1, 1, rows), lambda n: (ready[n], 0, 0)),
            pl.BlockSpec((2, HEAD_WIDTH, rows), lambda n: (ready[n], 0, 0)),
            pl.BlockSpec((2, 1, rows), lambda n: (ready[n], 0, 0)),
        ],
        out_specs=[
            pl.BlockSpec(
                (1, half, HEAD_WIDTH), lambda n: (place(n)[0], 0, rep[0] * heads + place(n)[1])
            ),
            pl.BlockSpec((1, half, HEAD_WIDTH), lambda n: (place(n)[0], 0, place(n)[1])),
        ],
    )
    when_any(count[0], pipeline, own_hbm, own_log_hbm, part_hbm, log_hbm, keep_hbm, send_hbm)


def merge(rep, ready, count, own, own_log, parts, logs, keep, send):
    heads, _, rows = own.shape
    smem = pl.BlockSpec(memory_space=pltpu.SMEM)
    anywhere = pl.BlockSpec(memory_space=pl.ANY)
    return pl.pallas_call(
        merge_kernel,
        in_specs=[smem] * 3 + [anywhere] * 6,
        out_specs=[anywhere, anywhere],
        out_shape=[
            jax.ShapeDtypeStruct(keep.shape, keep.dtype),
            jax.ShapeDtypeStruct(send.shape, send.dtype),
        ],
        input_output_aliases={7: 0, 8: 1},
        cost_estimate=pl.CostEstimate(
            flops=heads * rows * HEAD_WIDTH * 8,
            transcendentals=heads * rows * 3,
            bytes_accessed=heads * rows * HEAD_WIDTH * 10,
        ),
        name="merge_parts",
    )(rep.reshape(1), ready, count.reshape(1), own, own_log, parts, logs, keep, send)


def final_kernel(
    rep,
    table,
    count,
    q_hbm,
    k_hbm,
    v_hbm,
    own_hbm,
    own_log_hbm,
    part_in,
    log_in,
    keep_in,
    send_in,
    part_hbm,
    log_hbm,
    keep_hbm,
    send_hbm,
    step,
    held,
    held_log,
):
    rows = q_hbm.shape[1]
    half = rows // 2
    heads = send_hbm.shape[2] // HEAD_WIDTH
    step[0] = 0

    def attend(
        q_ref,
        k_ref,
        v_ref,
        own_ref,
        own_log_ref,
        other_ref,
        other_log_ref,
        part_ref,
        log_ref,
        keep_ref,
        send_ref,
    ):
        part, log = attend_tile(q_ref[0], k_ref[...], v_ref[...])
        second = table[6, step[0]] == 1
        other = jnp.where(second, held[...], other_ref[0])
        other_log = jnp.where(second, held_log[...], other_log_ref[0])
        keep_ref[0], send_ref[0] = merged_rows(
            rep[0], own_ref[0], own_log_ref[0], part, log, other, other_log
        )
        part_ref[0], log_ref[0] = part, log
        held[...], held_log[...] = part, log
        step[0] += 1

    tile = pl.BlockSpec((BLOCK_TOKENS, HEAD_WIDTH), lambda n: (table[1, n], table[2, n]))
    wide = (1, HEAD_WIDTH, rows)
    pipeline = pltpu.emit_pipeline(
        attend,
        grid=(count[0],),
        in_specs=[
            pl.BlockSpec((1, rows, HEAD_WIDTH), lambda n: (table[3, n], 0, table[4, n])),
            tile,
            tile,
            pl.BlockSpec(wide, lambda n: (table[3, n] * heads + table[4, n], 0, 0)),
            pl.BlockSpec((1, 1, rows), lambda n: (table[3, n] * heads + table[4, n], 0, 0)),
            pl.BlockSpec(wide, lambda n: (table[5, n], 0, 0)),
            pl.BlockSpec((1, 1, rows), lambda n: (table[5, n], 0, 0)),
        ],
        out_specs=[
            pl.BlockSpec(wide, lambda n: (table[0, n], 0, 0)),
            pl.BlockSpec((1, 1, rows), lambda n: (table[0, n], 0, 0)),
            pl.BlockSpec(
                (1, half, HEAD_WIDTH), lambda n: (table[3, n], 0, rep[0] * heads + table[4, n])
            ),
            pl.BlockSpec((1, half, HEAD_WIDTH), lambda n: (table[3, n], 0, table[4, n])),
        ],
    )
    when_any(
        count[0],
        pipeline,
        q_hbm,
        k_hbm,
        v_hbm,
        own_hbm,
        own_log_hbm,
        part_hbm,
        log_hbm,
        part_hbm,
        log_hbm,
        keep_hbm,
        send_hbm,
    )


def final_attention(rep, table, count, queries, keys, values, own, own_log, state):
    rows = queries.shape[1]
    expected = own.shape[0] // 8
    smem = pl.BlockSpec(memory_space=pltpu.SMEM)
    anywhere = pl.BlockSpec(memory_space=pl.ANY)
    return pl.pallas_call(
        final_kernel,
        in_specs=[smem] * 3 + [anywhere] * 9,
        out_specs=[anywhere] * 4,
        out_shape=[jax.ShapeDtypeStruct(value.shape, value.dtype) for value in state],
        scratch_shapes=[
            pltpu.SMEM((1,), jnp.int32),
            pltpu.VMEM((HEAD_WIDTH, rows), jnp.bfloat16),
            pltpu.VMEM((1, rows), jnp.float32),
        ],
        input_output_aliases={8: 0, 9: 1, 10: 2, 11: 3},
        cost_estimate=pl.CostEstimate(
            flops=expected * rows * BLOCK_TOKENS * HEAD_WIDTH * 4,
            transcendentals=expected * rows * BLOCK_TOKENS,
            bytes_accessed=expected * rows * HEAD_WIDTH * 18,
        ),
        name="final_attention",
    )(rep.reshape(1), table, count.reshape(1), queries, keys, values, own, own_log, *state)


def half_kernel(rep, from_ref, to_ref):
    to_ref[...] = from_ref[...]


def columns_kept(value, rep, size):
    rows = value.shape[0]
    return pl.pallas_call(
        half_kernel,
        grid_spec=pltpu.PrefetchScalarGridSpec(
            num_scalar_prefetch=1,
            grid=(rows // BLOCK_TOKENS,),
            in_specs=[pl.BlockSpec((BLOCK_TOKENS, size), lambda n, r: (n, r[0]))],
            out_specs=pl.BlockSpec((BLOCK_TOKENS, size), lambda n, r: (n, 0)),
        ),
        out_shape=jax.ShapeDtypeStruct((rows, size), value.dtype),
        cost_estimate=pl.CostEstimate(
            flops=0, transcendentals=0, bytes_accessed=rows * size * 4
        ),
        name="columns_kept",
    )(rep.reshape(1), value)


def ring_order(count):
    return list(range(0, count, 2)) + list(range(count - 1, 0, -2))


def compacted(mask, columns, spare):
    place = jnp.cumsum(mask.astype(jnp.int32), axis=1) - 1
    slot = jnp.arange(mask.shape[1])
    chosen = mask[:, :, None] & (place[:, :, None] == slot[None, None, :])
    filled = jnp.sum(jnp.where(chosen[:, None], columns[None, :, :, None], 0), axis=2)
    counts = jnp.sum(mask.astype(jnp.int32), axis=1)
    empty = (slot[None, :] >= counts[:, None])[:, None, :]
    return jnp.where(empty, spare[None, :, None], filled), counts


def body(queries, prefill_keys, prefill_values, context_keys, context_values, picks):
    local_count, _, full_width = queries.shape
    rep_size = lax.axis_size("rep")
    ctx_size = lax.axis_size("ctx")
    rep_index = lax.axis_index("rep")
    ctx_index = lax.axis_index("ctx")
    width = full_width // rep_size
    key_width = prefill_keys.shape[2] // rep_size
    heads = width // HEAD_WIDTH
    head_grouping = width // key_width
    blocks_here = context_keys.shape[0] // BLOCK_TOKENS
    items = 2 * local_count * heads
    swap = [(0, 1), (1, 0)]

    def columns_of(value, which, size):
        return lax.dynamic_slice_in_dim(value, which * size, size, axis=value.ndim - 1)

    own_shard = (
        columns_kept(context_keys, rep_index, key_width),
        columns_kept(context_values, rep_index, key_width),
    )
    order = ring_order(ctx_size)
    onward = [(order[n], order[(n + 1) % ctx_size]) for n in range(ctx_size)]
    backward = [(target, source) for source, target in onward]

    def hop(value, pairs):
        return lax.ppermute(value, "ctx", pairs)

    shards = {0: own_shard}
    ahead, behind = own_shard, own_shard
    full_steps = (ctx_size - 1) // 2
    for step in range(1, full_steps + 1):
        ahead = (hop(ahead[0], onward), hop(ahead[1], onward))
        behind = (hop(behind[0], backward), hop(behind[1], backward))
        shards[-step], shards[step] = ahead, behind
    step = full_steps + 1
    piece = context_keys.shape[0] // PIECES
    last_pieces = [
        (
            hop(ahead[0][n * piece : (n + 1) * piece], onward),
            hop(behind[1][n * piece : (n + 1) * piece], backward),
        )
        for n in range(PIECES)
    ]

    other = rep_size - 1 - rep_index

    def all_rows(value, size):
        kept = columns_of(value, rep_index, size)
        came = lax.ppermute(columns_of(value, other, size), "rep", swap)
        return jnp.where(
            rep_index == 0,
            jnp.concatenate([kept, came], axis=1),
            jnp.concatenate([came, kept], axis=1),
        )

    block_queries = all_rows(queries, width)
    block_keys = all_rows(prefill_keys, key_width)
    block_values = all_rows(prefill_values, key_width)

    position_of = [0] * ctx_size
    for position, device in enumerate(order):
        position_of[device] = position
    here = jnp.array(position_of, jnp.int32)[ctx_index]
    distances = sorted(shards, key=abs)
    wanted = jnp.array(order, jnp.int32)[
        (here + jnp.array([*distances, ctx_size // 2], jnp.int32)) % ctx_size
    ]
    mine = lax.dynamic_slice_in_dim(picks[:, :, :2], rep_index * heads, heads, axis=1).reshape(-1)
    place = jnp.arange(items)
    head = place // 2 % heads
    holders = mine // blocks_here
    tile = mine - holders * blocks_here
    facts = [head // head_grouping, place // (2 * heads), head]
    tables, counts = compacted(
        holders[None, :] == wanted[:-1, None],
        jnp.stack([place, tile, *facts]),
        jnp.zeros((5,), jnp.int32),
    )
    tiles = blocks_here // PIECES
    waits = holders == wanted[-1]
    inside = waits[None, :] & (tile[None, :] // tiles == jnp.arange(PIECES)[:, None])
    both = jnp.any(jnp.all(inside.reshape(PIECES, -1, 2), axis=2), axis=0)
    both = jnp.stack([both, both], axis=1).reshape(-1)
    last_tables, last_counts = compacted(
        inside,
        jnp.stack(
            [
                place,
                tile % tiles,
                *facts,
                jnp.where(both, items, place + 1 - 2 * (place % 2)),
                jnp.where(both, place % 2, 0),
            ]
        ),
        jnp.zeros((7,), jnp.int32),
    )
    ready, ready_counts = compacted(
        ~jnp.any(waits.reshape(1, -1, 2), axis=2),
        jnp.arange(items // 2)[None],
        jnp.zeros((1,), jnp.int32),
    )

    own, own_log, parts, logs, keep, send = own_attention(
        block_queries, block_keys, block_values, head_grouping, full_width
    )
    for n, distance in enumerate(distances):
        keys, values = shards[distance]
        parts, logs = pick_attention(tables[n], counts[n], block_queries, keys, values, parts, logs)
    keep, send = merge(
        rep_index, ready[0, 0], ready_counts[0], own, own_log, parts, logs, keep, send
    )
    state = (parts, logs, keep, send)
    for n, (keys, values) in enumerate(last_pieces):
        state = final_attention(
            rep_index,
            last_tables[n],
            last_counts[n],
            block_queries,
            keys,
            values,
            own,
            own_log,
            state,
        )
    arriving = lax.ppermute(state[3], "rep", swap)
    return lax.dynamic_update_slice_in_dim(state[2], arriving, other * width, axis=2)


def solution(mesh):
    return jax.shard_map(
        body,
        mesh=mesh,
        in_specs=(
            P(("groups", "ctx"), "rep", "head"),
            P(("groups", "ctx"), "rep", "head"),
            P(("groups", "ctx"), "rep", "head"),
            P(("groups", "ctx"), "head"),
            P(("groups", "ctx"), "head"),
            P(("groups", "ctx"), "head", None),
        ),
        out_specs=P(("groups", "ctx"), "rep", "head"),
        check_vma=False,
    )
```

```python
import jax
import jax.numpy as jnp
from jax import lax
from jax.experimental import pallas as pl
from jax.experimental.pallas import tpu as pltpu
from jax.sharding import PartitionSpec as P


HEAD_WIDTH = 128
BLOCK_TOKENS = 512
SCALE = HEAD_WIDTH ** (-0.5)
LOG2E = 1.4426950408889634
NEGATIVE = -1e30
PIECES = 2


def scores_by_key(keys, queries):
    return lax.dot_general(
        keys, queries, (((1,), (1,)), ((), ())), preferred_element_type=jnp.float32
    )


def mix_by_width(values, weights):
    return lax.dot_general(
        values,
        weights.astype(jnp.bfloat16),
        (((0,), (0,)), ((), ())),
        preferred_element_type=jnp.float32,
    )


def own_kernel(q_ref, k_ref, v_ref, part_ref, log_ref, *unwritten):
    half = q_ref.shape[1] // 2
    visible = lax.broadcasted_iota(jnp.int32, (half, half), 0) <= lax.broadcasted_iota(
        jnp.int32, (half, half), 1
    )
    early_keys, late_keys = k_ref[0, :half], k_ref[0, half:]
    early_queries, late_queries = q_ref[0, :half], q_ref[0, half:]

    first = jnp.where(visible, scores_by_key(early_keys, early_queries), NEGATIVE)
    highest = jnp.max(first, axis=0, keepdims=True)
    weights = jnp.exp2((first - highest) * (SCALE * LOG2E))
    total = jnp.sum(weights, axis=0, keepdims=True)
    part_ref[0, :, :half] = mix_by_width(v_ref[0, :half], weights) / total
    log_ref[0, :, :half] = highest * SCALE + jnp.log(total)

    before = scores_by_key(early_keys, late_queries)
    within = jnp.where(visible, scores_by_key(late_keys, late_queries), NEGATIVE)
    highest = jnp.maximum(
        jnp.max(before, axis=0, keepdims=True), jnp.max(within, axis=0, keepdims=True)
    )
    before = jnp.exp2((before - highest) * (SCALE * LOG2E))
    within = jnp.exp2((within - highest) * (SCALE * LOG2E))
    total = jnp.sum(before, axis=0, keepdims=True) + jnp.sum(within, axis=0, keepdims=True)
    mixed = mix_by_width(v_ref[0, :half], before) + mix_by_width(v_ref[0, half:], within)
    part_ref[0, :, half:] = mixed / total
    log_ref[0, :, half:] = highest * SCALE + jnp.log(total)


def own_attention(queries, keys, values, head_grouping, full_width):
    blocks, rows, width = queries.shape
    heads = width // HEAD_WIDTH
    count = blocks * heads
    items = 2 * count
    query_spec = pl.BlockSpec((1, rows, HEAD_WIDTH), lambda n: (lax.div(n, heads), 0, lax.rem(n, heads)))
    key_spec = pl.BlockSpec(
        (1, rows, HEAD_WIDTH), lambda n: (lax.div(n, heads), 0, lax.div(lax.rem(n, heads), head_grouping))
    )
    return pl.pallas_call(
        own_kernel,
        grid=(count,),
        in_specs=[query_spec, key_spec, key_spec],
        out_specs=[
            pl.BlockSpec((1, HEAD_WIDTH, rows), lambda n: (n, 0, 0)),
            pl.BlockSpec((1, 1, rows), lambda n: (n, 0, 0)),
        ]
        + [pl.BlockSpec(memory_space=pl.ANY)] * 4,
        out_shape=[
            jax.ShapeDtypeStruct((count, HEAD_WIDTH, rows), jnp.float32),
            jax.ShapeDtypeStruct((count, 1, rows), jnp.float32),
            jax.ShapeDtypeStruct((items + 2, HEAD_WIDTH, rows), jnp.bfloat16),
            jax.ShapeDtypeStruct((items + 2, 1, rows), jnp.float32),
            jax.ShapeDtypeStruct((blocks, rows // 2, full_width), jnp.bfloat16),
            jax.ShapeDtypeStruct((blocks, rows // 2, width), jnp.bfloat16),
        ],
        cost_estimate=pl.CostEstimate(
            flops=count * rows * rows * HEAD_WIDTH * 4,
            transcendentals=count * rows * rows,
            bytes_accessed=count * rows * HEAD_WIDTH * 8,
        ),
        name="own_attention",
    )(queries, keys, values)


def attend_tile(queries, keys, values):
    scores = scores_by_key(keys, queries)
    highest = jnp.max(scores, axis=0, keepdims=True)
    weights = jnp.exp2((scores - highest) * (SCALE * LOG2E))
    total = jnp.sum(weights, axis=0, keepdims=True)
    part = (mix_by_width(values, weights) / total).astype(jnp.bfloat16)
    return part, highest * SCALE + jnp.log(total)


def when_any(count, pipeline, *arrays):
    @pl.when(count > 0)
    def _():
        pipeline(*arrays)


def pick_kernel(table, count, q_hbm, k_hbm, v_hbm, part_in, log_in, part_hbm, log_hbm):
    rows = q_hbm.shape[1]

    def attend(q_ref, k_ref, v_ref, part_ref, log_ref):
        part_ref[0], log_ref[0] = attend_tile(q_ref[0], k_ref[...], v_ref[...])

    tile = pl.BlockSpec((BLOCK_TOKENS, HEAD_WIDTH), lambda n: (table[1, n], table[2, n]))
    pipeline = pltpu.emit_pipeline(
        attend,
        grid=(count[0],),
        in_specs=[
            pl.BlockSpec((1, rows, HEAD_WIDTH), lambda n: (table[3, n], 0, table[4, n])),
            tile,
            tile,
        ],
        out_specs=[
            pl.BlockSpec((1, HEAD_WIDTH, rows), lambda n: (table[0, n], 0, 0)),
            pl.BlockSpec((1, 1, rows), lambda n: (table[0, n], 0, 0)),
        ],
    )
    when_any(count[0], pipeline, q_hbm, k_hbm, v_hbm, part_hbm, log_hbm)


def pick_attention(table, count, queries, keys, values, parts, logs):
    blocks, rows, width = queries.shape
    expected = 2 * blocks * (width // HEAD_WIDTH) // 8
    smem = pl.BlockSpec(memory_space=pltpu.SMEM)
    anywhere = pl.BlockSpec(memory_space=pl.ANY)
    return pl.pallas_call(
        pick_kernel,
        in_specs=[smem, smem] + [anywhere] * 5,
        out_specs=[anywhere, anywhere],
        out_shape=[
            jax.ShapeDtypeStruct(parts.shape, parts.dtype),
            jax.ShapeDtypeStruct(logs.shape, logs.dtype),
        ],
        input_output_aliases={5: 0, 6: 1},
        cost_estimate=pl.CostEstimate(
            flops=expected * rows * BLOCK_TOKENS * HEAD_WIDTH * 4,
            transcendentals=expected * rows * BLOCK_TOKENS,
            bytes_accessed=expected * rows * HEAD_WIDTH * 8,
        ),
        name="pick_attention",
    )(table, count.reshape(1), queries, keys, values, parts, logs)


def merged_rows(rep, own, own_log, first, first_log, second, second_log):
    half = own.shape[1] // 2
    top = jnp.maximum(own_log, jnp.maximum(first_log, second_log))
    own_share = jnp.exp(own_log - top)
    first_share = jnp.exp(first_log - top)
    second_share = jnp.exp(second_log - top)
    merged = (
        own_share * own
        + first_share * first.astype(jnp.float32)
        + second_share * second.astype(jnp.float32)
    ) / (own_share + first_share + second_share)
    early = merged[:, :half].T.astype(jnp.bfloat16)
    late = merged[:, half:].T.astype(jnp.bfloat16)
    return jnp.where(rep == 0, early, late), jnp.where(rep == 0, late, early)


def merge_kernel(
    rep, ready, count, own_hbm, own_log_hbm, part_hbm, log_hbm, keep_in, send_in, keep_hbm, send_hbm
):
    rows = own_hbm.shape[2]
    half = rows // 2
    heads = send_hbm.shape[2] // HEAD_WIDTH

    def combine(own_ref, own_log_ref, part_ref, log_ref, keep_ref, send_ref):
        keep_ref[0], send_ref[0] = merged_rows(
            rep[0], own_ref[0], own_log_ref[0], part_ref[0], log_ref[0], part_ref[1], log_ref[1]
        )

    def place(n):
        return lax.div(ready[n], heads), lax.rem(ready[n], heads)

    pipeline = pltpu.emit_pipeline(
        combine,
        grid=(count[0],),
        in_specs=[
            pl.BlockSpec((1, HEAD_WIDTH, rows), lambda n: (ready[n], 0, 0)),
            pl.BlockSpec((1, 1, rows), lambda n: (ready[n], 0, 0)),
            pl.BlockSpec((2, HEAD_WIDTH, rows), lambda n: (ready[n], 0, 0)),
            pl.BlockSpec((2, 1, rows), lambda n: (ready[n], 0, 0)),
        ],
        out_specs=[
            pl.BlockSpec(
                (1, half, HEAD_WIDTH), lambda n: (place(n)[0], 0, rep[0] * heads + place(n)[1])
            ),
            pl.BlockSpec((1, half, HEAD_WIDTH), lambda n: (place(n)[0], 0, place(n)[1])),
        ],
    )
    when_any(count[0], pipeline, own_hbm, own_log_hbm, part_hbm, log_hbm, keep_hbm, send_hbm)


def merge(rep, ready, count, own, own_log, parts, logs, keep, send):
    heads, _, rows = own.shape
    smem = pl.BlockSpec(memory_space=pltpu.SMEM)
    anywhere = pl.BlockSpec(memory_space=pl.ANY)
    return pl.pallas_call(
        merge_kernel,
        in_specs=[smem] * 3 + [anywhere] * 6,
        out_specs=[anywhere, anywhere],
        out_shape=[
            jax.ShapeDtypeStruct(keep.shape, keep.dtype),
            jax.ShapeDtypeStruct(send.shape, send.dtype),
        ],
        input_output_aliases={7: 0, 8: 1},
        cost_estimate=pl.CostEstimate(
            flops=heads * rows * HEAD_WIDTH * 8,
            transcendentals=heads * rows * 3,
            bytes_accessed=heads * rows * HEAD_WIDTH * 10,
        ),
        name="merge_parts",
    )(rep.reshape(1), ready, count.reshape(1), own, own_log, parts, logs, keep, send)


def final_kernel(
    rep,
    table,
    count,
    q_hbm,
    k_hbm,
    v_hbm,
    own_hbm,
    own_log_hbm,
    part_in,
    log_in,
    keep_in,
    send_in,
    part_hbm,
    log_hbm,
    keep_hbm,
    send_hbm,
    step,
    held,
    held_log,
):
    rows = q_hbm.shape[1]
    half = rows // 2
    heads = send_hbm.shape[2] // HEAD_WIDTH
    step[0] = 0

    def attend(
        q_ref,
        k_ref,
        v_ref,
        own_ref,
        own_log_ref,
        other_ref,
        other_log_ref,
        part_ref,
        log_ref,
        keep_ref,
        send_ref,
    ):
        part, log = attend_tile(q_ref[0], k_ref[...], v_ref[...])
        second = table[6, step[0]] == 1
        other = jnp.where(second, held[...], other_ref[0])
        other_log = jnp.where(second, held_log[...], other_log_ref[0])
        keep_ref[0], send_ref[0] = merged_rows(
            rep[0], own_ref[0], own_log_ref[0], part, log, other, other_log
        )
        part_ref[0], log_ref[0] = part, log
        held[...], held_log[...] = part, log
        step[0] += 1

    tile = pl.BlockSpec((BLOCK_TOKENS, HEAD_WIDTH), lambda n: (table[1, n], table[2, n]))
    wide = (1, HEAD_WIDTH, rows)
    pipeline = pltpu.emit_pipeline(
        attend,
        grid=(count[0],),
        in_specs=[
            pl.BlockSpec((1, rows, HEAD_WIDTH), lambda n: (table[3, n], 0, table[4, n])),
            tile,
            tile,
            pl.BlockSpec(wide, lambda n: (table[3, n] * heads + table[4, n], 0, 0)),
            pl.BlockSpec((1, 1, rows), lambda n: (table[3, n] * heads + table[4, n], 0, 0)),
            pl.BlockSpec(wide, lambda n: (table[5, n], 0, 0)),
            pl.BlockSpec((1, 1, rows), lambda n: (table[5, n], 0, 0)),
        ],
        out_specs=[
            pl.BlockSpec(wide, lambda n: (table[0, n], 0, 0)),
            pl.BlockSpec((1, 1, rows), lambda n: (table[0, n], 0, 0)),
            pl.BlockSpec(
                (1, half, HEAD_WIDTH), lambda n: (table[3, n], 0, rep[0] * heads + table[4, n])
            ),
            pl.BlockSpec((1, half, HEAD_WIDTH), lambda n: (table[3, n], 0, table[4, n])),
        ],
    )
    when_any(
        count[0],
        pipeline,
        q_hbm,
        k_hbm,
        v_hbm,
        own_hbm,
        own_log_hbm,
        part_hbm,
        log_hbm,
        part_hbm,
        log_hbm,
        keep_hbm,
        send_hbm,
    )


def final_attention(rep, table, count, queries, keys, values, own, own_log, state):
    rows = queries.shape[1]
    expected = own.shape[0] // 8
    smem = pl.BlockSpec(memory_space=pltpu.SMEM)
    anywhere = pl.BlockSpec(memory_space=pl.ANY)
    return pl.pallas_call(
        final_kernel,
        in_specs=[smem] * 3 + [anywhere] * 9,
        out_specs=[anywhere] * 4,
        out_shape=[jax.ShapeDtypeStruct(value.shape, value.dtype) for value in state],
        scratch_shapes=[
            pltpu.SMEM((1,), jnp.int32),
            pltpu.VMEM((HEAD_WIDTH, rows), jnp.bfloat16),
            pltpu.VMEM((1, rows), jnp.float32),
        ],
        input_output_aliases={8: 0, 9: 1, 10: 2, 11: 3},
        cost_estimate=pl.CostEstimate(
            flops=expected * rows * BLOCK_TOKENS * HEAD_WIDTH * 4,
            transcendentals=expected * rows * BLOCK_TOKENS,
            bytes_accessed=expected * rows * HEAD_WIDTH * 18,
        ),
        name="final_attention",
    )(rep.reshape(1), table, count.reshape(1), queries, keys, values, own, own_log, *state)


def half_kernel(rep, from_ref, to_ref):
    to_ref[...] = from_ref[...]


def columns_kept(value, rep, size):
    rows = value.shape[0]
    return pl.pallas_call(
        half_kernel,
        grid_spec=pltpu.PrefetchScalarGridSpec(
            num_scalar_prefetch=1,
            grid=(rows // BLOCK_TOKENS,),
            in_specs=[pl.BlockSpec((BLOCK_TOKENS, size), lambda n, r: (n, r[0]))],
            out_specs=pl.BlockSpec((BLOCK_TOKENS, size), lambda n, r: (n, 0)),
        ),
        out_shape=jax.ShapeDtypeStruct((rows, size), value.dtype),
        cost_estimate=pl.CostEstimate(
            flops=0, transcendentals=0, bytes_accessed=rows * size * 4
        ),
        name="columns_kept",
    )(rep.reshape(1), value)


def ring_order(count):
    return list(range(0, count, 2)) + list(range(count - 1, 0, -2))


def compacted(mask, columns, spare):
    place = jnp.cumsum(mask.astype(jnp.int32), axis=1) - 1
    slot = jnp.arange(mask.shape[1])
    chosen = mask[:, :, None] & (place[:, :, None] == slot[None, None, :])
    filled = jnp.sum(jnp.where(chosen[:, None], columns[None, :, :, None], 0), axis=2)
    counts = jnp.sum(mask.astype(jnp.int32), axis=1)
    empty = (slot[None, :] >= counts[:, None])[:, None, :]
    return jnp.where(empty, spare[None, :, None], filled), counts


def body(queries, prefill_keys, prefill_values, context_keys, context_values, picks):
    local_count, _, full_width = queries.shape
    rep_size = lax.axis_size("rep")
    ctx_size = lax.axis_size("ctx")
    rep_index = lax.axis_index("rep")
    ctx_index = lax.axis_index("ctx")
    width = full_width // rep_size
    key_width = prefill_keys.shape[2] // rep_size
    heads = width // HEAD_WIDTH
    head_grouping = width // key_width
    blocks_here = context_keys.shape[0] // BLOCK_TOKENS
    items = 2 * local_count * heads
    swap = [(0, 1), (1, 0)]

    def columns_of(value, which, size):
        return lax.dynamic_slice_in_dim(value, which * size, size, axis=value.ndim - 1)

    own_shard = (
        columns_kept(context_keys, rep_index, key_width),
        columns_kept(context_values, rep_index, key_width),
    )
    order = ring_order(ctx_size)
    onward = [(order[n], order[(n + 1) % ctx_size]) for n in range(ctx_size)]
    backward = [(target, source) for source, target in onward]

    def hop(value, pairs):
        return lax.ppermute(value, "ctx", pairs)

    shards = {0: own_shard}
    ahead, behind = own_shard, own_shard
    full_steps = (ctx_size - 1) // 2
    for step in range(1, full_steps + 1):
        ahead = (hop(ahead[0], onward), hop(ahead[1], onward))
        behind = (hop(behind[0], backward), hop(behind[1], backward))
        shards[-step], shards[step] = ahead, behind
    step = full_steps + 1
    piece = context_keys.shape[0] // PIECES
    last_pieces = [
        (
            hop(ahead[0][n * piece : (n + 1) * piece], onward),
            hop(behind[1][n * piece : (n + 1) * piece], backward),
        )
        for n in range(PIECES)
    ]

    other = rep_size - 1 - rep_index

    def all_rows(value, size):
        kept = columns_of(value, rep_index, size)
        came = lax.ppermute(columns_of(value, other, size), "rep", swap)
        return jnp.where(
            rep_index == 0,
            jnp.concatenate([kept, came], axis=1),
            jnp.concatenate([came, kept], axis=1),
        )

    block_queries = all_rows(queries, width)
    block_keys = all_rows(prefill_keys, key_width)
    block_values = all_rows(prefill_values, key_width)

    position_of = [0] * ctx_size
    for position, device in enumerate(order):
        position_of[device] = position
    here = jnp.array(position_of, jnp.int32)[ctx_index]
    distances = sorted(shards, key=abs)
    wanted = jnp.array(order, jnp.int32)[
        (here + jnp.array([*distances, ctx_size // 2], jnp.int32)) % ctx_size
    ]
    mine = lax.dynamic_slice_in_dim(picks[:, :, :2], rep_index * heads, heads, axis=1).reshape(-1)
    place = jnp.arange(items)
    head = place // 2 % heads
    holders = mine // blocks_here
    tile = mine - holders * blocks_here
    facts = [head // head_grouping, place // (2 * heads), head]
    tables, counts = compacted(
        holders[None, :] == wanted[:-3, None],
        jnp.stack([place, tile, *facts]),
        jnp.zeros((5,), jnp.int32),
    )
    tiles = blocks_here // PIECES
    piece_of = tile // tiles
    inside = jnp.concatenate(
        [
            holders[None, :] == wanted[-3:-1, None],
            (holders == wanted[-1])[None, :] & (piece_of[None, :] == jnp.arange(PIECES)[:, None]),
        ]
    )
    both = jnp.any(jnp.all(inside.reshape(2 + PIECES, -1, 2), axis=2), axis=0)
    both = jnp.stack([both, both], axis=1).reshape(-1)
    last_tables, last_counts = compacted(
        inside,
        jnp.stack(
            [
                place,
                jnp.where(holders == wanted[-1], tile - piece_of * tiles, tile),
                *facts,
                jnp.where(both, items, place + 1 - 2 * (place % 2)),
                jnp.where(both, place % 2, 0),
            ]
        ),
        jnp.zeros((7,), jnp.int32),
    )
    ready, ready_counts = compacted(
        ~jnp.any(inside.reshape(1, -1, items // 2, 2), axis=(1, 3)),
        jnp.arange(items // 2)[None],
        jnp.zeros((1,), jnp.int32),
    )

    own, own_log, parts, logs, keep, send = own_attention(
        block_queries, block_keys, block_values, head_grouping, full_width
    )
    for n, distance in enumerate(distances[:-2]):
        keys, values = shards[distance]
        parts, logs = pick_attention(tables[n], counts[n], block_queries, keys, values, parts, logs)
    keep, send = merge(
        rep_index, ready[0, 0], ready_counts[0], own, own_log, parts, logs, keep, send
    )
    state = (parts, logs, keep, send)
    late_arrivals = [shards[distance] for distance in distances[-2:]] + last_pieces
    for n, (keys, values) in enumerate(late_arrivals):
        state = final_attention(
            rep_index,
            last_tables[n],
            last_counts[n],
            block_queries,
            keys,
            values,
            own,
            own_log,
            state,
        )
    arriving = lax.ppermute(state[3], "rep", swap)
    return lax.dynamic_update_slice_in_dim(state[2], arriving, other * width, axis=2)


def solution(mesh):
    return jax.shard_map(
        body,
        mesh=mesh,
        in_specs=(
            P(("groups", "ctx"), "rep", "head"),
            P(("groups", "ctx"), "rep", "head"),
            P(("groups", "ctx"), "rep", "head"),
            P(("groups", "ctx"), "head"),
            P(("groups", "ctx"), "head"),
            P(("groups", "ctx"), "head", None),
        ),
        out_specs=P(("groups", "ctx"), "rep", "head"),
        check_vma=False,
    )
```

```python
import jax
import jax.numpy as jnp
from jax import lax
from jax.experimental import pallas as pl
from jax.experimental.pallas import tpu as pltpu
from jax.sharding import PartitionSpec as P


HEAD_WIDTH = 128
BLOCK_TOKENS = 512
SCALE = HEAD_WIDTH ** (-0.5)
LOG2E = 1.4426950408889634
NEGATIVE = -1e30


def fetched(shape, index_map):
    return pl.BlockSpec(shape, index_map, pipeline_mode=pl.Buffered(3))


def scores_by_key(keys, queries):
    return lax.dot_general(
        keys, queries, (((1,), (1,)), ((), ())), preferred_element_type=jnp.float32
    )


def mix_by_width(values, weights):
    return lax.dot_general(
        values,
        weights.astype(jnp.bfloat16),
        (((0,), (0,)), ((), ())),
        preferred_element_type=jnp.float32,
    )


def own_kernel(q_ref, k_ref, v_ref, part_ref, log_ref, *unwritten):
    half = q_ref.shape[1] // 2
    visible = lax.broadcasted_iota(jnp.int32, (half, half), 0) <= lax.broadcasted_iota(
        jnp.int32, (half, half), 1
    )
    early_keys, late_keys = k_ref[0, :half], k_ref[0, half:]
    early_queries, late_queries = q_ref[0, :half], q_ref[0, half:]

    first = jnp.where(visible, scores_by_key(early_keys, early_queries), NEGATIVE)
    highest = jnp.max(first, axis=0, keepdims=True)
    weights = jnp.exp2((first - highest) * (SCALE * LOG2E))
    total = jnp.sum(weights, axis=0, keepdims=True)
    part_ref[0, :, :half] = mix_by_width(v_ref[0, :half], weights) / total
    log_ref[0, :, :half] = highest * SCALE + jnp.log(total)

    before = scores_by_key(early_keys, late_queries)
    within = jnp.where(visible, scores_by_key(late_keys, late_queries), NEGATIVE)
    highest = jnp.maximum(
        jnp.max(before, axis=0, keepdims=True), jnp.max(within, axis=0, keepdims=True)
    )
    before = jnp.exp2((before - highest) * (SCALE * LOG2E))
    within = jnp.exp2((within - highest) * (SCALE * LOG2E))
    total = jnp.sum(before, axis=0, keepdims=True) + jnp.sum(within, axis=0, keepdims=True)
    mixed = mix_by_width(v_ref[0, :half], before) + mix_by_width(v_ref[0, half:], within)
    part_ref[0, :, half:] = mixed / total
    log_ref[0, :, half:] = highest * SCALE + jnp.log(total)


def own_attention(queries, keys, values, head_grouping, full_width):
    blocks, rows, width = queries.shape
    heads = width // HEAD_WIDTH
    count = blocks * heads
    items = 2 * count
    query_spec = pl.BlockSpec((1, rows, HEAD_WIDTH), lambda n: (lax.div(n, heads), 0, lax.rem(n, heads)))
    key_spec = pl.BlockSpec(
        (1, rows, HEAD_WIDTH), lambda n: (lax.div(n, heads), 0, lax.div(lax.rem(n, heads), head_grouping))
    )
    return pl.pallas_call(
        own_kernel,
        grid=(count,),
        in_specs=[query_spec, key_spec, key_spec],
        out_specs=[
            pl.BlockSpec((1, HEAD_WIDTH, rows), lambda n: (n, 0, 0)),
            pl.BlockSpec((1, 1, rows), lambda n: (n, 0, 0)),
        ]
        + [pl.BlockSpec(memory_space=pl.ANY)] * 4,
        out_shape=[
            jax.ShapeDtypeStruct((count, HEAD_WIDTH, rows), jnp.float32),
            jax.ShapeDtypeStruct((count, 1, rows), jnp.float32),
            jax.ShapeDtypeStruct((items + 2, HEAD_WIDTH, rows), jnp.bfloat16),
            jax.ShapeDtypeStruct((items + 2, 1, rows), jnp.float32),
            jax.ShapeDtypeStruct((blocks, rows // 2, full_width), jnp.bfloat16),
            jax.ShapeDtypeStruct((blocks, rows // 2, width), jnp.bfloat16),
        ],
        cost_estimate=pl.CostEstimate(
            flops=count * rows * rows * HEAD_WIDTH * 4,
            transcendentals=count * rows * rows,
            bytes_accessed=count * rows * HEAD_WIDTH * 8,
        ),
        name="own_attention",
    )(queries, keys, values)


def attend_tile(queries, keys, values):
    scores = scores_by_key(keys, queries)
    highest = jnp.max(scores, axis=0, keepdims=True)
    weights = jnp.exp2((scores - highest) * (SCALE * LOG2E))
    total = jnp.sum(weights, axis=0, keepdims=True)
    part = (mix_by_width(values, weights) / total).astype(jnp.bfloat16)
    return part, highest * SCALE + jnp.log(total)


def when_any(count, pipeline, *arrays):
    @pl.when(count > 0)
    def _():
        pipeline(*arrays)


def pick_kernel(table, count, q_hbm, k_hbm, v_hbm, part_in, log_in, part_hbm, log_hbm):
    rows = q_hbm.shape[1]

    def attend(q_ref, k_ref, v_ref, part_ref, log_ref):
        part_ref[0], log_ref[0] = attend_tile(q_ref[0], k_ref[...], v_ref[...])

    tile = fetched((BLOCK_TOKENS, HEAD_WIDTH), lambda n: (table[1, n], table[2, n]))
    pipeline = pltpu.emit_pipeline(
        attend,
        grid=(count[0],),
        in_specs=[
            fetched((1, rows, HEAD_WIDTH), lambda n: (table[3, n], 0, table[4, n])),
            tile,
            tile,
        ],
        out_specs=[
            pl.BlockSpec((1, HEAD_WIDTH, rows), lambda n: (table[0, n], 0, 0)),
            pl.BlockSpec((1, 1, rows), lambda n: (table[0, n], 0, 0)),
        ],
    )
    when_any(count[0], pipeline, q_hbm, k_hbm, v_hbm, part_hbm, log_hbm)


def pick_attention(table, count, queries, keys, values, parts, logs):
    blocks, rows, width = queries.shape
    expected = 2 * blocks * (width // HEAD_WIDTH) // 8
    smem = pl.BlockSpec(memory_space=pltpu.SMEM)
    anywhere = pl.BlockSpec(memory_space=pl.ANY)
    return pl.pallas_call(
        pick_kernel,
        in_specs=[smem, smem] + [anywhere] * 5,
        out_specs=[anywhere, anywhere],
        out_shape=[
            jax.ShapeDtypeStruct(parts.shape, parts.dtype),
            jax.ShapeDtypeStruct(logs.shape, logs.dtype),
        ],
        input_output_aliases={5: 0, 6: 1},
        cost_estimate=pl.CostEstimate(
            flops=expected * rows * BLOCK_TOKENS * HEAD_WIDTH * 4,
            transcendentals=expected * rows * BLOCK_TOKENS,
            bytes_accessed=expected * rows * HEAD_WIDTH * 8,
        ),
        name="pick_attention",
    )(table, count.reshape(1), queries, keys, values, parts, logs)


def merged_rows(rep, own, own_log, first, first_log, second, second_log):
    half = own.shape[1] // 2
    top = jnp.maximum(own_log, jnp.maximum(first_log, second_log))
    own_share = jnp.exp(own_log - top)
    first_share = jnp.exp(first_log - top)
    second_share = jnp.exp(second_log - top)
    merged = (
        own_share * own
        + first_share * first.astype(jnp.float32)
        + second_share * second.astype(jnp.float32)
    ) / (own_share + first_share + second_share)
    early = merged[:, :half].T.astype(jnp.bfloat16)
    late = merged[:, half:].T.astype(jnp.bfloat16)
    return jnp.where(rep == 0, early, late), jnp.where(rep == 0, late, early)


def merge_kernel(
    rep, ready, count, own_hbm, own_log_hbm, part_hbm, log_hbm, keep_in, send_in, keep_hbm, send_hbm
):
    rows = own_hbm.shape[2]
    half = rows // 2
    heads = send_hbm.shape[2] // HEAD_WIDTH

    def combine(own_ref, own_log_ref, part_ref, log_ref, keep_ref, send_ref):
        keep_ref[0], send_ref[0] = merged_rows(
            rep[0], own_ref[0], own_log_ref[0], part_ref[0], log_ref[0], part_ref[1], log_ref[1]
        )

    def place(n):
        return lax.div(ready[n], heads), lax.rem(ready[n], heads)

    pipeline = pltpu.emit_pipeline(
        combine,
        grid=(count[0],),
        in_specs=[
            fetched((1, HEAD_WIDTH, rows), lambda n: (ready[n], 0, 0)),
            fetched((1, 1, rows), lambda n: (ready[n], 0, 0)),
            fetched((2, HEAD_WIDTH, rows), lambda n: (ready[n], 0, 0)),
            fetched((2, 1, rows), lambda n: (ready[n], 0, 0)),
        ],
        out_specs=[
            pl.BlockSpec(
                (1, half, HEAD_WIDTH), lambda n: (place(n)[0], 0, rep[0] * heads + place(n)[1])
            ),
            pl.BlockSpec((1, half, HEAD_WIDTH), lambda n: (place(n)[0], 0, place(n)[1])),
        ],
    )
    when_any(count[0], pipeline, own_hbm, own_log_hbm, part_hbm, log_hbm, keep_hbm, send_hbm)


def merge(rep, ready, count, own, own_log, parts, logs, keep, send):
    heads, _, rows = own.shape
    smem = pl.BlockSpec(memory_space=pltpu.SMEM)
    anywhere = pl.BlockSpec(memory_space=pl.ANY)
    return pl.pallas_call(
        merge_kernel,
        in_specs=[smem] * 3 + [anywhere] * 6,
        out_specs=[anywhere, anywhere],
        out_shape=[
            jax.ShapeDtypeStruct(keep.shape, keep.dtype),
            jax.ShapeDtypeStruct(send.shape, send.dtype),
        ],
        input_output_aliases={7: 0, 8: 1},
        cost_estimate=pl.CostEstimate(
            flops=heads * rows * HEAD_WIDTH * 8,
            transcendentals=heads * rows * 3,
            bytes_accessed=heads * rows * HEAD_WIDTH * 10,
        ),
        name="merge_parts",
    )(rep.reshape(1), ready, count.reshape(1), own, own_log, parts, logs, keep, send)


def final_kernel(
    rep,
    table,
    count,
    q_hbm,
    k_hbm,
    v_hbm,
    own_hbm,
    own_log_hbm,
    part_in,
    log_in,
    keep_in,
    send_in,
    part_hbm,
    log_hbm,
    keep_hbm,
    send_hbm,
    step,
    held,
    held_log,
):
    rows = q_hbm.shape[1]
    half = rows // 2
    heads = send_hbm.shape[2] // HEAD_WIDTH
    step[0] = 0

    def attend(
        q_ref,
        k_ref,
        v_ref,
        own_ref,
        own_log_ref,
        other_ref,
        other_log_ref,
        part_ref,
        log_ref,
        keep_ref,
        send_ref,
    ):
        part, log = attend_tile(q_ref[0], k_ref[...], v_ref[...])
        second = table[6, step[0]] == 1
        other = jnp.where(second, held[...], other_ref[0])
        other_log = jnp.where(second, held_log[...], other_log_ref[0])
        keep_ref[0], send_ref[0] = merged_rows(
            rep[0], own_ref[0], own_log_ref[0], part, log, other, other_log
        )
        part_ref[0], log_ref[0] = part, log
        held[...], held_log[...] = part, log
        step[0] += 1

    tile = fetched((BLOCK_TOKENS, HEAD_WIDTH), lambda n: (table[1, n], table[2, n]))
    wide = (1, HEAD_WIDTH, rows)
    pipeline = pltpu.emit_pipeline(
        attend,
        grid=(count[0],),
        in_specs=[
            fetched((1, rows, HEAD_WIDTH), lambda n: (table[3, n], 0, table[4, n])),
            tile,
            tile,
            fetched(wide, lambda n: (table[3, n] * heads + table[4, n], 0, 0)),
            fetched((1, 1, rows), lambda n: (table[3, n] * heads + table[4, n], 0, 0)),
            fetched(wide, lambda n: (table[5, n], 0, 0)),
            fetched((1, 1, rows), lambda n: (table[5, n], 0, 0)),
        ],
        out_specs=[
            pl.BlockSpec(wide, lambda n: (table[0, n], 0, 0)),
            pl.BlockSpec((1, 1, rows), lambda n: (table[0, n], 0, 0)),
            pl.BlockSpec(
                (1, half, HEAD_WIDTH), lambda n: (table[3, n], 0, rep[0] * heads + table[4, n])
            ),
            pl.BlockSpec((1, half, HEAD_WIDTH), lambda n: (table[3, n], 0, table[4, n])),
        ],
    )
    when_any(
        count[0],
        pipeline,
        q_hbm,
        k_hbm,
        v_hbm,
        own_hbm,
        own_log_hbm,
        part_hbm,
        log_hbm,
        part_hbm,
        log_hbm,
        keep_hbm,
        send_hbm,
    )


def final_attention(rep, table, count, queries, keys, values, own, own_log, state):
    rows = queries.shape[1]
    expected = own.shape[0] // 8
    smem = pl.BlockSpec(memory_space=pltpu.SMEM)
    anywhere = pl.BlockSpec(memory_space=pl.ANY)
    return pl.pallas_call(
        final_kernel,
        in_specs=[smem] * 3 + [anywhere] * 9,
        out_specs=[anywhere] * 4,
        out_shape=[jax.ShapeDtypeStruct(value.shape, value.dtype) for value in state],
        scratch_shapes=[
            pltpu.SMEM((1,), jnp.int32),
            pltpu.VMEM((HEAD_WIDTH, rows), jnp.bfloat16),
            pltpu.VMEM((1, rows), jnp.float32),
        ],
        input_output_aliases={8: 0, 9: 1, 10: 2, 11: 3},
        cost_estimate=pl.CostEstimate(
            flops=expected * rows * BLOCK_TOKENS * HEAD_WIDTH * 4,
            transcendentals=expected * rows * BLOCK_TOKENS,
            bytes_accessed=expected * rows * HEAD_WIDTH * 18,
        ),
        name="final_attention",
    )(rep.reshape(1), table, count.reshape(1), queries, keys, values, own, own_log, *state)


def kept_kernel(rep, from_ref, to_ref, held, arrived, left):
    size = to_ref.shape[1]
    columns = pl.ds(pl.multiple_of(rep[0] * size, HEAD_WIDTH), size)
    pieces = [pl.ds(n * BLOCK_TOKENS, BLOCK_TOKENS) for n in range(to_ref.shape[0] // BLOCK_TOKENS)]
    incoming = [
        pltpu.make_async_copy(from_ref.at[piece, columns], held.at[piece], arrived.at[n])
        for n, piece in enumerate(pieces)
    ]
    outgoing = [
        pltpu.make_async_copy(held.at[piece], to_ref.at[piece], left.at[n])
        for n, piece in enumerate(pieces)
    ]
    for copy in incoming:
        copy.start()
    for copy, onward in zip(incoming, outgoing):
        copy.wait()
        onward.start()
    for copy in outgoing:
        copy.wait()


def columns_kept(value, rep, size):
    rows = value.shape[0]
    pieces = rows // BLOCK_TOKENS
    return pl.pallas_call(
        kept_kernel,
        in_specs=[pl.BlockSpec(memory_space=pltpu.SMEM), pl.BlockSpec(memory_space=pl.ANY)],
        out_specs=pl.BlockSpec(memory_space=pl.ANY),
        out_shape=jax.ShapeDtypeStruct((rows, size), value.dtype),
        scratch_shapes=[
            pltpu.VMEM((rows, size), value.dtype),
            pltpu.SemaphoreType.DMA((pieces,)),
            pltpu.SemaphoreType.DMA((pieces,)),
        ],
        cost_estimate=pl.CostEstimate(
            flops=0, transcendentals=0, bytes_accessed=rows * size * 4
        ),
        name="columns_kept",
    )(rep.reshape(1), value)


def piece_starts(blocks):
    starts = [0]
    while blocks - starts[-1] > 1:
        starts.append(starts[-1] + (blocks - starts[-1] + 1) // 2)
    return starts


def ring_order(count):
    return list(range(0, count, 2)) + list(range(count - 1, 0, -2))


def compacted(mask, columns, spare):
    place = jnp.cumsum(mask.astype(jnp.int32), axis=1) - 1
    slot = jnp.arange(mask.shape[1])
    chosen = mask[:, :, None] & (place[:, :, None] == slot[None, None, :])
    filled = jnp.sum(jnp.where(chosen[:, None], columns[None, :, :, None], 0), axis=2)
    counts = jnp.sum(mask.astype(jnp.int32), axis=1)
    empty = (slot[None, :] >= counts[:, None])[:, None, :]
    return jnp.where(empty, spare[None, :, None], filled), counts


def body(queries, prefill_keys, prefill_values, context_keys, context_values, picks):
    local_count, _, full_width = queries.shape
    rep_size = lax.axis_size("rep")
    ctx_size = lax.axis_size("ctx")
    rep_index = lax.axis_index("rep")
    ctx_index = lax.axis_index("ctx")
    width = full_width // rep_size
    key_width = prefill_keys.shape[2] // rep_size
    heads = width // HEAD_WIDTH
    head_grouping = width // key_width
    blocks_here = context_keys.shape[0] // BLOCK_TOKENS
    items = 2 * local_count * heads
    swap = [(0, 1), (1, 0)]

    def columns_of(value, which, size):
        return lax.dynamic_slice_in_dim(value, which * size, size, axis=value.ndim - 1)

    own_shard = (
        columns_kept(context_keys, rep_index, key_width),
        columns_kept(context_values, rep_index, key_width),
    )
    order = ring_order(ctx_size)
    onward = [(order[n], order[(n + 1) % ctx_size]) for n in range(ctx_size)]
    backward = [(target, source) for source, target in onward]

    def hop(value, pairs):
        return lax.ppermute(value, "ctx", pairs)

    shards = {0: own_shard}
    ahead, behind = own_shard, own_shard
    full_steps = (ctx_size - 1) // 2
    for step in range(1, full_steps + 1):
        ahead = (hop(ahead[0], onward), hop(ahead[1], onward))
        behind = (hop(behind[0], backward), hop(behind[1], backward))
        shards[-step], shards[step] = ahead, behind
    step = full_steps + 1
    starts = piece_starts(blocks_here)
    last_pieces = []
    for first, end in zip(starts, starts[1:] + [blocks_here]):
        rows = slice(first * BLOCK_TOKENS, end * BLOCK_TOKENS)
        last_pieces.append((hop(ahead[0][rows], onward), hop(behind[1][rows], backward)))

    other = rep_size - 1 - rep_index

    def all_rows(value, size):
        kept = columns_of(value, rep_index, size)
        came = lax.ppermute(columns_of(value, other, size), "rep", swap)
        return jnp.where(
            rep_index == 0,
            jnp.concatenate([kept, came], axis=1),
            jnp.concatenate([came, kept], axis=1),
        )

    block_queries = all_rows(queries, width)
    block_keys = all_rows(prefill_keys, key_width)
    block_values = all_rows(prefill_values, key_width)

    position_of = [0] * ctx_size
    for position, device in enumerate(order):
        position_of[device] = position
    here = jnp.array(position_of, jnp.int32)[ctx_index]
    distances = sorted(shards, key=abs)
    wanted = jnp.array(order, jnp.int32)[
        (here + jnp.array([*distances, ctx_size // 2], jnp.int32)) % ctx_size
    ]
    mine = lax.dynamic_slice_in_dim(picks[:, :, :2], rep_index * heads, heads, axis=1).reshape(-1)
    place = jnp.arange(items)
    head = place // 2 % heads
    holders = mine // blocks_here
    tile = mine - holders * blocks_here
    facts = [head // head_grouping, place // (2 * heads), head]
    tables, counts = compacted(
        holders[None, :] == wanted[:-3, None],
        jnp.stack([place, tile, *facts]),
        jnp.zeros((5,), jnp.int32),
    )
    first_tiles = jnp.array(starts, jnp.int32)
    piece_of = jnp.sum(tile[:, None] >= first_tiles[None, 1:], axis=1)
    piece_start = jnp.sum(
        jnp.where(piece_of[:, None] == jnp.arange(len(starts))[None, :], first_tiles[None, :], 0),
        axis=1,
    )
    inside = jnp.concatenate(
        [
            holders[None, :] == wanted[-3:-1, None],
            (holders == wanted[-1])[None, :] & (piece_of[None, :] == jnp.arange(len(starts))[:, None]),
        ]
    )
    both = jnp.any(jnp.all(inside.reshape(2 + len(starts), -1, 2), axis=2), axis=0)
    both = jnp.stack([both, both], axis=1).reshape(-1)
    last_tables, last_counts = compacted(
        inside,
        jnp.stack(
            [
                place,
                jnp.where(holders == wanted[-1], tile - piece_start, tile),
                *facts,
                jnp.where(both, items, place + 1 - 2 * (place % 2)),
                jnp.where(both, place % 2, 0),
            ]
        ),
        jnp.zeros((7,), jnp.int32),
    )
    ready, ready_counts = compacted(
        ~jnp.any(inside.reshape(1, -1, items // 2, 2), axis=(1, 3)),
        jnp.arange(items // 2)[None],
        jnp.zeros((1,), jnp.int32),
    )

    own, own_log, parts, logs, keep, send = own_attention(
        block_queries, block_keys, block_values, head_grouping, full_width
    )
    for n, distance in enumerate(distances[:-2]):
        keys, values = shards[distance]
        parts, logs = pick_attention(tables[n], counts[n], block_queries, keys, values, parts, logs)
    keep, send = merge(
        rep_index, ready[0, 0], ready_counts[0], own, own_log, parts, logs, keep, send
    )
    state = (parts, logs, keep, send)
    late_arrivals = [shards[distance] for distance in distances[-2:]] + last_pieces
    for n, (keys, values) in enumerate(late_arrivals):
        state = final_attention(
            rep_index,
            last_tables[n],
            last_counts[n],
            block_queries,
            keys,
            values,
            own,
            own_log,
            state,
        )
    arriving = lax.ppermute(state[3], "rep", swap)
    return lax.dynamic_update_slice_in_dim(state[2], arriving, other * width, axis=2)


def solution(mesh):
    return jax.shard_map(
        body,
        mesh=mesh,
        in_specs=(
            P(("groups", "ctx"), "rep", "head"),
            P(("groups", "ctx"), "rep", "head"),
            P(("groups", "ctx"), "rep", "head"),
            P(("groups", "ctx"), "head"),
            P(("groups", "ctx"), "head"),
            P(("groups", "ctx"), "head", None),
        ),
        out_specs=P(("groups", "ctx"), "rep", "head"),
        check_vma=False,
    )
```

```python
import functools

import jax
import jax.numpy as jnp
from jax import lax
from jax.experimental import pallas as pl
from jax.experimental.pallas import tpu as pltpu
from jax.sharding import PartitionSpec as P


HEAD_WIDTH = 128
BLOCK_TOKENS = 512
SCALE = HEAD_WIDTH ** (-0.5)
LOG2E = 1.4426950408889634
NEGATIVE = -1e30


def fetched(shape, index_map):
    return pl.BlockSpec(shape, index_map, pipeline_mode=pl.Buffered(3))


def scores_by_key(keys, queries):
    return lax.dot_general(
        keys, queries, (((1,), (1,)), ((), ())), preferred_element_type=jnp.float32
    )


def mix_by_width(values, weights):
    return lax.dot_general(
        values,
        weights.astype(jnp.bfloat16),
        (((0,), (0,)), ((), ())),
        preferred_element_type=jnp.float32,
    )


def own_kernel(q_ref, k_ref, v_ref, part_ref, log_ref, *unwritten):
    half = q_ref.shape[1] // 2
    visible = lax.broadcasted_iota(jnp.int32, (half, half), 0) <= lax.broadcasted_iota(
        jnp.int32, (half, half), 1
    )
    early_keys, late_keys = k_ref[0, :half], k_ref[0, half:]
    early_queries, late_queries = q_ref[0, :half], q_ref[0, half:]

    first = jnp.where(visible, scores_by_key(early_keys, early_queries), NEGATIVE)
    highest = jnp.max(first, axis=0, keepdims=True)
    weights = jnp.exp2((first - highest) * (SCALE * LOG2E))
    total = jnp.sum(weights, axis=0, keepdims=True)
    part_ref[0, :, :half] = mix_by_width(v_ref[0, :half], weights) / total
    log_ref[0, :, :half] = highest * SCALE + jnp.log(total)

    before = scores_by_key(early_keys, late_queries)
    within = jnp.where(visible, scores_by_key(late_keys, late_queries), NEGATIVE)
    highest = jnp.maximum(
        jnp.max(before, axis=0, keepdims=True), jnp.max(within, axis=0, keepdims=True)
    )
    before = jnp.exp2((before - highest) * (SCALE * LOG2E))
    within = jnp.exp2((within - highest) * (SCALE * LOG2E))
    total = jnp.sum(before, axis=0, keepdims=True) + jnp.sum(within, axis=0, keepdims=True)
    mixed = mix_by_width(v_ref[0, :half], before) + mix_by_width(v_ref[0, half:], within)
    part_ref[0, :, half:] = mixed / total
    log_ref[0, :, half:] = highest * SCALE + jnp.log(total)


def own_attention(queries, keys, values, head_grouping, full_width):
    blocks, rows, width = queries.shape
    heads = width // HEAD_WIDTH
    count = blocks * heads
    items = 2 * count
    query_spec = pl.BlockSpec((1, rows, HEAD_WIDTH), lambda n: (lax.div(n, heads), 0, lax.rem(n, heads)))
    key_spec = pl.BlockSpec(
        (1, rows, HEAD_WIDTH), lambda n: (lax.div(n, heads), 0, lax.div(lax.rem(n, heads), head_grouping))
    )
    return pl.pallas_call(
        own_kernel,
        grid=(count,),
        in_specs=[query_spec, key_spec, key_spec],
        out_specs=[
            pl.BlockSpec((1, HEAD_WIDTH, rows), lambda n: (n, 0, 0)),
            pl.BlockSpec((1, 1, rows), lambda n: (n, 0, 0)),
        ]
        + [pl.BlockSpec(memory_space=pl.ANY)] * 4,
        out_shape=[
            jax.ShapeDtypeStruct((count, HEAD_WIDTH, rows), jnp.float32),
            jax.ShapeDtypeStruct((count, 1, rows), jnp.float32),
            jax.ShapeDtypeStruct((items + 2, HEAD_WIDTH, rows), jnp.bfloat16),
            jax.ShapeDtypeStruct((items + 2, 1, rows), jnp.float32),
            jax.ShapeDtypeStruct((blocks, rows // 2, full_width), jnp.bfloat16),
            jax.ShapeDtypeStruct((blocks, rows // 2, width), jnp.bfloat16),
        ],
        cost_estimate=pl.CostEstimate(
            flops=count * rows * rows * HEAD_WIDTH * 4,
            transcendentals=count * rows * rows,
            bytes_accessed=count * rows * HEAD_WIDTH * 8,
        ),
        name="own_attention",
    )(queries, keys, values)


def attend_tile(queries, keys, values):
    scores = scores_by_key(keys, queries)
    highest = jnp.max(scores, axis=0, keepdims=True)
    weights = jnp.exp2((scores - highest) * (SCALE * LOG2E))
    total = jnp.sum(weights, axis=0, keepdims=True)
    part = (mix_by_width(values, weights) / total).astype(jnp.bfloat16)
    return part, highest * SCALE + jnp.log(total)


def when_any(count, pipeline, *arrays):
    @pl.when(count > 0)
    def _():
        pipeline(*arrays)


def pick_kernel(row, table, count, q_hbm, k_hbm, v_hbm, part_in, log_in, part_hbm, log_hbm):
    rows = q_hbm.shape[1]

    def attend(q_ref, k_ref, v_ref, part_ref, log_ref):
        part_ref[0], log_ref[0] = attend_tile(q_ref[0], k_ref[...], v_ref[...])

    tile = fetched((BLOCK_TOKENS, HEAD_WIDTH), lambda n: (table[row, 1, n], table[row, 2, n]))
    pipeline = pltpu.emit_pipeline(
        attend,
        grid=(count[row],),
        in_specs=[
            fetched((1, rows, HEAD_WIDTH), lambda n: (table[row, 3, n], 0, table[row, 4, n])),
            tile,
            tile,
        ],
        out_specs=[
            pl.BlockSpec((1, HEAD_WIDTH, rows), lambda n: (table[row, 0, n], 0, 0)),
            pl.BlockSpec((1, 1, rows), lambda n: (table[row, 0, n], 0, 0)),
        ],
    )
    when_any(count[row], pipeline, q_hbm, k_hbm, v_hbm, part_hbm, log_hbm)


def pick_attention(row, table, count, queries, keys, values, parts, logs):
    blocks, rows, width = queries.shape
    expected = 2 * blocks * (width // HEAD_WIDTH) // 8
    smem = pl.BlockSpec(memory_space=pltpu.SMEM)
    anywhere = pl.BlockSpec(memory_space=pl.ANY)
    return pl.pallas_call(
        functools.partial(pick_kernel, row),
        in_specs=[smem, smem] + [anywhere] * 5,
        out_specs=[anywhere, anywhere],
        out_shape=[
            jax.ShapeDtypeStruct(parts.shape, parts.dtype),
            jax.ShapeDtypeStruct(logs.shape, logs.dtype),
        ],
        input_output_aliases={5: 0, 6: 1},
        cost_estimate=pl.CostEstimate(
            flops=expected * rows * BLOCK_TOKENS * HEAD_WIDTH * 4,
            transcendentals=expected * rows * BLOCK_TOKENS,
            bytes_accessed=expected * rows * HEAD_WIDTH * 8,
        ),
        name="pick_attention",
    )(table, count, queries, keys, values, parts, logs)


def merged_rows(rep, own, own_log, first, first_log, second, second_log):
    half = own.shape[1] // 2
    top = jnp.maximum(own_log, jnp.maximum(first_log, second_log))
    own_share = jnp.exp(own_log - top)
    first_share = jnp.exp(first_log - top)
    second_share = jnp.exp(second_log - top)
    merged = (
        own_share * own
        + first_share * first.astype(jnp.float32)
        + second_share * second.astype(jnp.float32)
    ) / (own_share + first_share + second_share)
    early = merged[:, :half].T.astype(jnp.bfloat16)
    late = merged[:, half:].T.astype(jnp.bfloat16)
    return jnp.where(rep == 0, early, late), jnp.where(rep == 0, late, early)


def merge_kernel(
    rep, ready, count, own_hbm, own_log_hbm, part_hbm, log_hbm, keep_in, send_in, keep_hbm, send_hbm
):
    rows = own_hbm.shape[2]
    half = rows // 2
    heads = send_hbm.shape[2] // HEAD_WIDTH

    def combine(own_ref, own_log_ref, part_ref, log_ref, keep_ref, send_ref):
        keep_ref[0], send_ref[0] = merged_rows(
            rep[0], own_ref[0], own_log_ref[0], part_ref[0], log_ref[0], part_ref[1], log_ref[1]
        )

    def place(n):
        return lax.div(ready[n], heads), lax.rem(ready[n], heads)

    pipeline = pltpu.emit_pipeline(
        combine,
        grid=(count[0],),
        in_specs=[
            fetched((1, HEAD_WIDTH, rows), lambda n: (ready[n], 0, 0)),
            fetched((1, 1, rows), lambda n: (ready[n], 0, 0)),
            fetched((2, HEAD_WIDTH, rows), lambda n: (ready[n], 0, 0)),
            fetched((2, 1, rows), lambda n: (ready[n], 0, 0)),
        ],
        out_specs=[
            pl.BlockSpec(
                (1, half, HEAD_WIDTH), lambda n: (place(n)[0], 0, rep[0] * heads + place(n)[1])
            ),
            pl.BlockSpec((1, half, HEAD_WIDTH), lambda n: (place(n)[0], 0, place(n)[1])),
        ],
    )
    when_any(count[0], pipeline, own_hbm, own_log_hbm, part_hbm, log_hbm, keep_hbm, send_hbm)


def merge(rep, ready, count, own, own_log, parts, logs, keep, send):
    heads, _, rows = own.shape
    smem = pl.BlockSpec(memory_space=pltpu.SMEM)
    anywhere = pl.BlockSpec(memory_space=pl.ANY)
    return pl.pallas_call(
        merge_kernel,
        in_specs=[smem] * 3 + [anywhere] * 6,
        out_specs=[anywhere, anywhere],
        out_shape=[
            jax.ShapeDtypeStruct(keep.shape, keep.dtype),
            jax.ShapeDtypeStruct(send.shape, send.dtype),
        ],
        input_output_aliases={7: 0, 8: 1},
        cost_estimate=pl.CostEstimate(
            flops=heads * rows * HEAD_WIDTH * 8,
            transcendentals=heads * rows * 3,
            bytes_accessed=heads * rows * HEAD_WIDTH * 10,
        ),
        name="merge_parts",
    )(rep.reshape(1), ready, count.reshape(1), own, own_log, parts, logs, keep, send)


def final_kernel(first_row, groups, rep, table, count, q_hbm, *refs):
    arrivals, refs = refs[: 2 * groups], refs[2 * groups :]
    own_hbm, own_log_hbm, _, _, _, _, part_hbm, log_hbm, keep_hbm, send_hbm = refs[:10]
    step, held, held_log = refs[10:]
    rows = q_hbm.shape[1]
    half = rows // 2
    heads = send_hbm.shape[2] // HEAD_WIDTH
    wide = (1, HEAD_WIDTH, rows)

    def run(row, k_hbm, v_hbm):
        def attend(
            q_ref,
            k_ref,
            v_ref,
            own_ref,
            own_log_ref,
            other_ref,
            other_log_ref,
            part_ref,
            log_ref,
            keep_ref,
            send_ref,
        ):
            part, log = attend_tile(q_ref[0], k_ref[...], v_ref[...])
            second = table[row, 6, step[0]] == 1
            other = jnp.where(second, held[...], other_ref[0])
            other_log = jnp.where(second, held_log[...], other_log_ref[0])
            keep_ref[0], send_ref[0] = merged_rows(
                rep[0], own_ref[0], own_log_ref[0], part, log, other, other_log
            )
            part_ref[0], log_ref[0] = part, log
            held[...], held_log[...] = part, log
            step[0] += 1

        def at(column):
            return lambda n: (table[row, column, n], 0, 0)

        def own_at(n):
            return (table[row, 3, n] * heads + table[row, 4, n], 0, 0)

        tile = fetched(
            (BLOCK_TOKENS, HEAD_WIDTH), lambda n: (table[row, 1, n], table[row, 2, n])
        )
        step[0] = 0
        pipeline = pltpu.emit_pipeline(
            attend,
            grid=(count[row],),
            in_specs=[
                fetched(
                    (1, rows, HEAD_WIDTH), lambda n: (table[row, 3, n], 0, table[row, 4, n])
                ),
                tile,
                tile,
                fetched(wide, own_at),
                fetched((1, 1, rows), own_at),
                fetched(wide, at(5)),
                fetched((1, 1, rows), at(5)),
            ],
            out_specs=[
                pl.BlockSpec(wide, at(0)),
                pl.BlockSpec((1, 1, rows), at(0)),
                pl.BlockSpec(
                    (1, half, HEAD_WIDTH),
                    lambda n: (table[row, 3, n], 0, rep[0] * heads + table[row, 4, n]),
                ),
                pl.BlockSpec(
                    (1, half, HEAD_WIDTH), lambda n: (table[row, 3, n], 0, table[row, 4, n])
                ),
            ],
        )
        when_any(
            count[row],
            pipeline,
            q_hbm,
            k_hbm,
            v_hbm,
            own_hbm,
            own_log_hbm,
            part_hbm,
            log_hbm,
            part_hbm,
            log_hbm,
            keep_hbm,
            send_hbm,
        )

    for n in range(groups):
        run(first_row + n, arrivals[2 * n], arrivals[2 * n + 1])


def final_attention(first_row, rep, table, count, queries, arrivals, own, own_log, state):
    rows = queries.shape[1]
    groups = len(arrivals)
    expected = own.shape[0] * groups // 8
    smem = pl.BlockSpec(memory_space=pltpu.SMEM)
    anywhere = pl.BlockSpec(memory_space=pl.ANY)
    flat = [array for pair in arrivals for array in pair]
    return pl.pallas_call(
        functools.partial(final_kernel, first_row, groups),
        in_specs=[smem] * 3 + [anywhere] * (7 + len(flat)),
        out_specs=[anywhere] * 4,
        out_shape=[jax.ShapeDtypeStruct(value.shape, value.dtype) for value in state],
        scratch_shapes=[
            pltpu.SMEM((1,), jnp.int32),
            pltpu.VMEM((HEAD_WIDTH, rows), jnp.bfloat16),
            pltpu.VMEM((1, rows), jnp.float32),
        ],
        input_output_aliases={6 + len(flat) + n: n for n in range(4)},
        cost_estimate=pl.CostEstimate(
            flops=expected * rows * BLOCK_TOKENS * HEAD_WIDTH * 4,
            transcendentals=expected * rows * BLOCK_TOKENS,
            bytes_accessed=expected * rows * HEAD_WIDTH * 18,
        ),
        name="final_attention",
    )(rep.reshape(1), table, count, queries, *flat, own, own_log, *state)


def kept_kernel(rep, from_ref, to_ref, held, arrived, left):
    size = to_ref.shape[1]
    columns = pl.ds(pl.multiple_of(rep[0] * size, HEAD_WIDTH), size)
    pieces = [pl.ds(n * BLOCK_TOKENS, BLOCK_TOKENS) for n in range(to_ref.shape[0] // BLOCK_TOKENS)]
    incoming = [
        pltpu.make_async_copy(from_ref.at[piece, columns], held.at[piece], arrived.at[n])
        for n, piece in enumerate(pieces)
    ]
    outgoing = [
        pltpu.make_async_copy(held.at[piece], to_ref.at[piece], left.at[n])
        for n, piece in enumerate(pieces)
    ]
    for copy in incoming:
        copy.start()
    for copy, onward in zip(incoming, outgoing):
        copy.wait()
        onward.start()
    for copy in outgoing:
        copy.wait()


def columns_kept(value, rep, size):
    rows = value.shape[0]
    pieces = rows // BLOCK_TOKENS
    return pl.pallas_call(
        kept_kernel,
        in_specs=[pl.BlockSpec(memory_space=pltpu.SMEM), pl.BlockSpec(memory_space=pl.ANY)],
        out_specs=pl.BlockSpec(memory_space=pl.ANY),
        out_shape=jax.ShapeDtypeStruct((rows, size), value.dtype),
        scratch_shapes=[
            pltpu.VMEM((rows, size), value.dtype),
            pltpu.SemaphoreType.DMA((pieces,)),
            pltpu.SemaphoreType.DMA((pieces,)),
        ],
        cost_estimate=pl.CostEstimate(
            flops=0, transcendentals=0, bytes_accessed=rows * size * 4
        ),
        name="columns_kept",
    )(rep.reshape(1), value)


def piece_starts(blocks):
    starts = [0]
    while blocks - starts[-1] > 1:
        starts.append(starts[-1] + (blocks - starts[-1] + 1) // 2)
    return starts


def ring_order(count):
    return list(range(0, count, 2)) + list(range(count - 1, 0, -2))


def compacted(mask, columns, spare):
    place = jnp.cumsum(mask.astype(jnp.int32), axis=1) - 1
    slot = jnp.arange(mask.shape[1])
    chosen = mask[:, :, None] & (place[:, :, None] == slot[None, None, :])
    filled = jnp.sum(jnp.where(chosen[:, None], columns[None, :, :, None], 0), axis=2)
    counts = jnp.sum(mask.astype(jnp.int32), axis=1)
    empty = (slot[None, :] >= counts[:, None])[:, None, :]
    return jnp.where(empty, spare[None, :, None], filled), counts


def body(queries, prefill_keys, prefill_values, context_keys, context_values, picks):
    local_count, _, full_width = queries.shape
    rep_size = lax.axis_size("rep")
    ctx_size = lax.axis_size("ctx")
    rep_index = lax.axis_index("rep")
    ctx_index = lax.axis_index("ctx")
    width = full_width // rep_size
    key_width = prefill_keys.shape[2] // rep_size
    heads = width // HEAD_WIDTH
    head_grouping = width // key_width
    blocks_here = context_keys.shape[0] // BLOCK_TOKENS
    items = 2 * local_count * heads
    swap = [(0, 1), (1, 0)]

    def columns_of(value, which, size):
        return lax.dynamic_slice_in_dim(value, which * size, size, axis=value.ndim - 1)

    own_shard = (
        columns_kept(context_keys, rep_index, key_width),
        columns_kept(context_values, rep_index, key_width),
    )
    order = ring_order(ctx_size)
    onward = [(order[n], order[(n + 1) % ctx_size]) for n in range(ctx_size)]
    backward = [(target, source) for source, target in onward]

    def hop(value, pairs):
        return lax.ppermute(value, "ctx", pairs)

    shards = {0: own_shard}
    ahead, behind = own_shard, own_shard
    full_steps = (ctx_size - 1) // 2
    for step in range(1, full_steps):
        ahead = (hop(ahead[0], onward), hop(ahead[1], onward))
        behind = (hop(behind[0], backward), hop(behind[1], backward))
        shards[-step], shards[step] = ahead, behind
    starts = piece_starts(blocks_here)
    cut = starts[1] * BLOCK_TOKENS

    def hop_in_parts(shard, pairs):
        keys, values = shard
        return [
            (hop(keys[:cut], pairs), hop(values[:cut], pairs)),
            (hop(keys[cut:], pairs), hop(values[cut:], pairs)),
        ]

    ahead, behind = hop_in_parts(ahead, onward), hop_in_parts(behind, backward)
    step = full_steps + 1
    last_pieces = []
    for n, (first, end) in enumerate(zip(starts, starts[1:] + [blocks_here])):
        part = min(n, 1)
        rows = slice((first - part * starts[1]) * BLOCK_TOKENS, (end - part * starts[1]) * BLOCK_TOKENS)
        last_pieces.append(
            (hop(ahead[part][0][rows], onward), hop(behind[part][1][rows], backward))
        )

    other = rep_size - 1 - rep_index

    def all_rows(value, size):
        kept = columns_of(value, rep_index, size)
        came = lax.ppermute(columns_of(value, other, size), "rep", swap)
        return jnp.where(
            rep_index == 0,
            jnp.concatenate([kept, came], axis=1),
            jnp.concatenate([came, kept], axis=1),
        )

    block_queries = all_rows(queries, width)
    block_keys = all_rows(prefill_keys, key_width)
    block_values = all_rows(prefill_values, key_width)

    position_of = [0] * ctx_size
    for position, device in enumerate(order):
        position_of[device] = position
    here = jnp.array(position_of, jnp.int32)[ctx_index]
    distances = sorted(shards, key=abs)
    late_distances = [-full_steps, full_steps, ctx_size // 2]
    wanted = jnp.array(order, jnp.int32)[
        (here + jnp.array(distances + late_distances, jnp.int32)) % ctx_size
    ]
    mine = lax.dynamic_slice_in_dim(picks[:, :, :2], rep_index * heads, heads, axis=1).reshape(-1)
    place = jnp.arange(items)
    head = place // 2 % heads
    holders = mine // blocks_here
    tile = mine - holders * blocks_here
    facts = [head // head_grouping, place // (2 * heads), head]
    tables, counts = compacted(
        holders[None, :] == wanted[:-3, None],
        jnp.stack([place, tile, *facts]),
        jnp.zeros((5,), jnp.int32),
    )
    first_tiles = jnp.array(starts, jnp.int32)
    piece_of = jnp.sum(tile[:, None] >= first_tiles[None, 1:], axis=1)
    halfway = holders == wanted[-1]
    reached = jnp.where(halfway, piece_of, jnp.minimum(piece_of, 1))
    piece_start = jnp.sum(
        jnp.where(reached[:, None] == jnp.arange(len(starts))[None, :], first_tiles[None, :], 0),
        axis=1,
    )
    sides = holders[None, :] == wanted[-3:-1, None]
    inside = jnp.concatenate(
        [
            sides & (reached == 0)[None, :],
            sides & (reached == 1)[None, :],
            halfway[None, :] & (piece_of[None, :] == jnp.arange(len(starts))[:, None]),
        ]
    )
    both = jnp.any(jnp.all(inside.reshape(4 + len(starts), -1, 2), axis=2), axis=0)
    both = jnp.stack([both, both], axis=1).reshape(-1)
    last_tables, last_counts = compacted(
        inside,
        jnp.stack(
            [
                place,
                tile - piece_start,
                *facts,
                jnp.where(both, items, place + 1 - 2 * (place % 2)),
                jnp.where(both, place % 2, 0),
            ]
        ),
        jnp.zeros((7,), jnp.int32),
    )
    ready, ready_counts = compacted(
        ~jnp.any(inside.reshape(1, -1, items // 2, 2), axis=(1, 3)),
        jnp.arange(items // 2)[None],
        jnp.zeros((1,), jnp.int32),
    )

    own, own_log, parts, logs, keep, send = own_attention(
        block_queries, block_keys, block_values, head_grouping, full_width
    )
    for n, distance in enumerate(distances):
        keys, values = shards[distance]
        parts, logs = pick_attention(n, tables, counts, block_queries, keys, values, parts, logs)
    keep, send = merge(
        rep_index, ready[0, 0], ready_counts[0], own, own_log, parts, logs, keep, send
    )
    state = (parts, logs, keep, send)
    late_arrivals = [list(pair) for pair in zip(ahead, behind)] + [[pair] for pair in last_pieces]
    row = 0
    for arrivals in late_arrivals:
        state = final_attention(
            row,
            rep_index,
            last_tables,
            last_counts,
            block_queries,
            arrivals,
            own,
            own_log,
            state,
        )
        row += len(arrivals)
    arriving = lax.ppermute(state[3], "rep", swap)
    return lax.dynamic_update_slice_in_dim(state[2], arriving, other * width, axis=2)


def solution(mesh):
    return jax.shard_map(
        body,
        mesh=mesh,
        in_specs=(
            P(("groups", "ctx"), "rep", "head"),
            P(("groups", "ctx"), "rep", "head"),
            P(("groups", "ctx"), "rep", "head"),
            P(("groups", "ctx"), "head"),
            P(("groups", "ctx"), "head"),
            P(("groups", "ctx"), "head", None),
        ),
        out_specs=P(("groups", "ctx"), "rep", "head"),
        check_vma=False,
    )
```

```python
import functools

import jax
import jax.numpy as jnp
from jax import lax
from jax.experimental import pallas as pl
from jax.experimental.pallas import tpu as pltpu
from jax.sharding import PartitionSpec as P


HEAD_WIDTH = 128
BLOCK_TOKENS = 512
SCALE = HEAD_WIDTH ** (-0.5)
LOG2E = 1.4426950408889634
NEGATIVE = -1e30


def fetched(shape, index_map):
    return pl.BlockSpec(shape, index_map, pipeline_mode=pl.Buffered(3))


def scores_by_key(keys, queries):
    return lax.dot_general(
        keys, queries, (((1,), (1,)), ((), ())), preferred_element_type=jnp.float32
    )


def mix_by_width(values, weights):
    return lax.dot_general(
        values,
        weights.astype(jnp.bfloat16),
        (((0,), (0,)), ((), ())),
        preferred_element_type=jnp.float32,
    )


def own_kernel(q_ref, k_ref, v_ref, part_ref, log_ref, *unwritten):
    half = q_ref.shape[1] // 2
    visible = lax.broadcasted_iota(jnp.int32, (half, half), 0) <= lax.broadcasted_iota(
        jnp.int32, (half, half), 1
    )
    early_keys, late_keys = k_ref[0, :half], k_ref[0, half:]
    early_queries, late_queries = q_ref[0, :half], q_ref[0, half:]

    first = jnp.where(visible, scores_by_key(early_keys, early_queries), NEGATIVE)
    highest = jnp.max(first, axis=0, keepdims=True)
    weights = jnp.exp2((first - highest) * (SCALE * LOG2E))
    total = jnp.sum(weights, axis=0, keepdims=True)
    part_ref[0, :, :half] = (mix_by_width(v_ref[0, :half], weights) / total).astype(
        part_ref.dtype
    )
    log_ref[0, :, :half] = highest * SCALE + jnp.log(total)

    before = scores_by_key(early_keys, late_queries)
    within = jnp.where(visible, scores_by_key(late_keys, late_queries), NEGATIVE)
    highest = jnp.maximum(
        jnp.max(before, axis=0, keepdims=True), jnp.max(within, axis=0, keepdims=True)
    )
    before = jnp.exp2((before - highest) * (SCALE * LOG2E))
    within = jnp.exp2((within - highest) * (SCALE * LOG2E))
    total = jnp.sum(before, axis=0, keepdims=True) + jnp.sum(within, axis=0, keepdims=True)
    mixed = mix_by_width(v_ref[0, :half], before) + mix_by_width(v_ref[0, half:], within)
    part_ref[0, :, half:] = (mixed / total).astype(part_ref.dtype)
    log_ref[0, :, half:] = highest * SCALE + jnp.log(total)


def own_attention(queries, keys, values, head_grouping, full_width):
    blocks, rows, width = queries.shape
    heads = width // HEAD_WIDTH
    count = blocks * heads
    items = 2 * count
    query_spec = pl.BlockSpec((1, rows, HEAD_WIDTH), lambda n: (lax.div(n, heads), 0, lax.rem(n, heads)))
    key_spec = pl.BlockSpec(
        (1, rows, HEAD_WIDTH), lambda n: (lax.div(n, heads), 0, lax.div(lax.rem(n, heads), head_grouping))
    )
    return pl.pallas_call(
        own_kernel,
        grid=(count,),
        in_specs=[query_spec, key_spec, key_spec],
        out_specs=[
            pl.BlockSpec((1, HEAD_WIDTH, rows), lambda n: (n, 0, 0)),
            pl.BlockSpec((1, 1, rows), lambda n: (n, 0, 0)),
        ]
        + [pl.BlockSpec(memory_space=pl.ANY)] * 4,
        out_shape=[
            jax.ShapeDtypeStruct((count, HEAD_WIDTH, rows), jnp.bfloat16),
            jax.ShapeDtypeStruct((count, 1, rows), jnp.float32),
            jax.ShapeDtypeStruct((items + 2, HEAD_WIDTH, rows), jnp.bfloat16),
            jax.ShapeDtypeStruct((items + 2, 1, rows), jnp.float32),
            jax.ShapeDtypeStruct((blocks, rows // 2, full_width), jnp.bfloat16),
            jax.ShapeDtypeStruct((blocks, rows // 2, width), jnp.bfloat16),
        ],
        cost_estimate=pl.CostEstimate(
            flops=count * rows * rows * HEAD_WIDTH * 4,
            transcendentals=count * rows * rows,
            bytes_accessed=count * rows * HEAD_WIDTH * 8,
        ),
        name="own_attention",
    )(queries, keys, values)


def attend_tile(queries, keys, values):
    scores = scores_by_key(keys, queries)
    highest = jnp.max(scores, axis=0, keepdims=True)
    weights = jnp.exp2((scores - highest) * (SCALE * LOG2E))
    total = jnp.sum(weights, axis=0, keepdims=True)
    part = (mix_by_width(values, weights) / total).astype(jnp.bfloat16)
    return part, highest * SCALE + jnp.log(total)


def when_any(count, pipeline, *arrays):
    @pl.when(count > 0)
    def _():
        pipeline(*arrays)


def pick_kernel(row, table, count, q_hbm, k_hbm, v_hbm, part_in, log_in, part_hbm, log_hbm):
    rows = q_hbm.shape[1]

    def attend(q_ref, k_ref, v_ref, part_ref, log_ref):
        part_ref[0], log_ref[0] = attend_tile(q_ref[0], k_ref[...], v_ref[...])

    tile = fetched((BLOCK_TOKENS, HEAD_WIDTH), lambda n: (table[row, 1, n], table[row, 2, n]))
    pipeline = pltpu.emit_pipeline(
        attend,
        grid=(count[row],),
        in_specs=[
            fetched((1, rows, HEAD_WIDTH), lambda n: (table[row, 3, n], 0, table[row, 4, n])),
            tile,
            tile,
        ],
        out_specs=[
            pl.BlockSpec((1, HEAD_WIDTH, rows), lambda n: (table[row, 0, n], 0, 0)),
            pl.BlockSpec((1, 1, rows), lambda n: (table[row, 0, n], 0, 0)),
        ],
    )
    when_any(count[row], pipeline, q_hbm, k_hbm, v_hbm, part_hbm, log_hbm)


def pick_attention(row, table, count, queries, keys, values, parts, logs):
    blocks, rows, width = queries.shape
    expected = 2 * blocks * (width // HEAD_WIDTH) // 8
    smem = pl.BlockSpec(memory_space=pltpu.SMEM)
    anywhere = pl.BlockSpec(memory_space=pl.ANY)
    return pl.pallas_call(
        functools.partial(pick_kernel, row),
        in_specs=[smem, smem] + [anywhere] * 5,
        out_specs=[anywhere, anywhere],
        out_shape=[
            jax.ShapeDtypeStruct(parts.shape, parts.dtype),
            jax.ShapeDtypeStruct(logs.shape, logs.dtype),
        ],
        input_output_aliases={5: 0, 6: 1},
        cost_estimate=pl.CostEstimate(
            flops=expected * rows * BLOCK_TOKENS * HEAD_WIDTH * 4,
            transcendentals=expected * rows * BLOCK_TOKENS,
            bytes_accessed=expected * rows * HEAD_WIDTH * 8,
        ),
        name="pick_attention",
    )(table, count, queries, keys, values, parts, logs)


def merged_rows(rep, own, own_log, first, first_log, second, second_log):
    half = own.shape[1] // 2
    top = jnp.maximum(own_log, jnp.maximum(first_log, second_log))
    own_share = jnp.exp(own_log - top)
    first_share = jnp.exp(first_log - top)
    second_share = jnp.exp(second_log - top)
    merged = (
        own_share * own.astype(jnp.float32)
        + first_share * first.astype(jnp.float32)
        + second_share * second.astype(jnp.float32)
    ) / (own_share + first_share + second_share)
    early = merged[:, :half].T.astype(jnp.bfloat16)
    late = merged[:, half:].T.astype(jnp.bfloat16)
    return jnp.where(rep == 0, early, late), jnp.where(rep == 0, late, early)


def merge_kernel(
    rep, ready, count, own_hbm, own_log_hbm, part_hbm, log_hbm, keep_in, send_in, keep_hbm, send_hbm
):
    rows = own_hbm.shape[2]
    half = rows // 2
    heads = send_hbm.shape[2] // HEAD_WIDTH

    def combine(own_ref, own_log_ref, part_ref, log_ref, keep_ref, send_ref):
        keep_ref[0], send_ref[0] = merged_rows(
            rep[0], own_ref[0], own_log_ref[0], part_ref[0], log_ref[0], part_ref[1], log_ref[1]
        )

    def place(n):
        return lax.div(ready[n], heads), lax.rem(ready[n], heads)

    pipeline = pltpu.emit_pipeline(
        combine,
        grid=(count[0],),
        in_specs=[
            fetched((1, HEAD_WIDTH, rows), lambda n: (ready[n], 0, 0)),
            fetched((1, 1, rows), lambda n: (ready[n], 0, 0)),
            fetched((2, HEAD_WIDTH, rows), lambda n: (ready[n], 0, 0)),
            fetched((2, 1, rows), lambda n: (ready[n], 0, 0)),
        ],
        out_specs=[
            pl.BlockSpec(
                (1, half, HEAD_WIDTH), lambda n: (place(n)[0], 0, rep[0] * heads + place(n)[1])
            ),
            pl.BlockSpec((1, half, HEAD_WIDTH), lambda n: (place(n)[0], 0, place(n)[1])),
        ],
    )
    when_any(count[0], pipeline, own_hbm, own_log_hbm, part_hbm, log_hbm, keep_hbm, send_hbm)


def merge(rep, ready, count, own, own_log, parts, logs, keep, send):
    heads, _, rows = own.shape
    smem = pl.BlockSpec(memory_space=pltpu.SMEM)
    anywhere = pl.BlockSpec(memory_space=pl.ANY)
    return pl.pallas_call(
        merge_kernel,
        in_specs=[smem] * 3 + [anywhere] * 6,
        out_specs=[anywhere, anywhere],
        out_shape=[
            jax.ShapeDtypeStruct(keep.shape, keep.dtype),
            jax.ShapeDtypeStruct(send.shape, send.dtype),
        ],
        input_output_aliases={7: 0, 8: 1},
        cost_estimate=pl.CostEstimate(
            flops=heads * rows * HEAD_WIDTH * 8,
            transcendentals=heads * rows * 3,
            bytes_accessed=heads * rows * HEAD_WIDTH * 10,
        ),
        name="merge_parts",
    )(rep.reshape(1), ready, count.reshape(1), own, own_log, parts, logs, keep, send)


def final_kernel(first_row, groups, keeps_parts, rep, table, count, q_hbm, *refs):
    arrivals, refs = refs[: 2 * groups], refs[2 * groups :]
    own_hbm, own_log_hbm, _, _, _, _, part_hbm, log_hbm, keep_hbm, send_hbm = refs[:10]
    step, held, held_log = refs[10:]
    rows = q_hbm.shape[1]
    half = rows // 2
    heads = send_hbm.shape[2] // HEAD_WIDTH
    wide = (1, HEAD_WIDTH, rows)

    def run(row, k_hbm, v_hbm):
        def attend(
            q_ref,
            k_ref,
            v_ref,
            own_ref,
            own_log_ref,
            other_ref,
            other_log_ref,
            keep_ref,
            send_ref,
            *part_refs,
        ):
            part, log = attend_tile(q_ref[0], k_ref[...], v_ref[...])
            second = table[row, 6, step[0]] == 1
            other = jnp.where(second, held[...], other_ref[0])
            other_log = jnp.where(second, held_log[...], other_log_ref[0])
            keep_ref[0], send_ref[0] = merged_rows(
                rep[0], own_ref[0], own_log_ref[0], part, log, other, other_log
            )
            if keeps_parts:
                part_refs[0][0], part_refs[1][0] = part, log
            held[...], held_log[...] = part, log
            step[0] += 1

        def at(column):
            return lambda n: (table[row, column, n], 0, 0)

        def own_at(n):
            return (table[row, 3, n] * heads + table[row, 4, n], 0, 0)

        tile = fetched(
            (BLOCK_TOKENS, HEAD_WIDTH), lambda n: (table[row, 1, n], table[row, 2, n])
        )
        step[0] = 0
        pipeline = pltpu.emit_pipeline(
            attend,
            grid=(count[row],),
            in_specs=[
                fetched(
                    (1, rows, HEAD_WIDTH), lambda n: (table[row, 3, n], 0, table[row, 4, n])
                ),
                tile,
                tile,
                fetched(wide, own_at),
                fetched((1, 1, rows), own_at),
                fetched(wide, at(5)),
                fetched((1, 1, rows), at(5)),
            ],
            out_specs=[
                pl.BlockSpec(
                    (1, half, HEAD_WIDTH),
                    lambda n: (table[row, 3, n], 0, rep[0] * heads + table[row, 4, n]),
                ),
                pl.BlockSpec(
                    (1, half, HEAD_WIDTH), lambda n: (table[row, 3, n], 0, table[row, 4, n])
                ),
                pl.BlockSpec(wide, at(0)),
                pl.BlockSpec((1, 1, rows), at(0)),
            ][: 4 if keeps_parts else 2],
        )
        when_any(
            count[row],
            pipeline,
            q_hbm,
            k_hbm,
            v_hbm,
            own_hbm,
            own_log_hbm,
            part_hbm,
            log_hbm,
            *(keep_hbm, send_hbm, part_hbm, log_hbm)[: 4 if keeps_parts else 2],
        )

    for n in range(groups):
        run(first_row + n, arrivals[2 * n], arrivals[2 * n + 1])


def final_attention(first_row, keeps_parts, rep, table, count, queries, arrivals, own, own_log, state):
    rows = queries.shape[1]
    groups = len(arrivals)
    expected = own.shape[0] * groups // 8
    smem = pl.BlockSpec(memory_space=pltpu.SMEM)
    anywhere = pl.BlockSpec(memory_space=pl.ANY)
    flat = [array for pair in arrivals for array in pair]
    return pl.pallas_call(
        functools.partial(final_kernel, first_row, groups, keeps_parts),
        in_specs=[smem] * 3 + [anywhere] * (7 + len(flat)),
        out_specs=[anywhere] * 4,
        out_shape=[jax.ShapeDtypeStruct(value.shape, value.dtype) for value in state],
        scratch_shapes=[
            pltpu.SMEM((1,), jnp.int32),
            pltpu.VMEM((HEAD_WIDTH, rows), jnp.bfloat16),
            pltpu.VMEM((1, rows), jnp.float32),
        ],
        input_output_aliases={6 + len(flat) + n: n for n in range(4)},
        cost_estimate=pl.CostEstimate(
            flops=expected * rows * BLOCK_TOKENS * HEAD_WIDTH * 4,
            transcendentals=expected * rows * BLOCK_TOKENS,
            bytes_accessed=expected * rows * HEAD_WIDTH * 18,
        ),
        name="final_attention",
    )(rep.reshape(1), table, count, queries, *flat, own, own_log, *state)


def kept_kernel(rep, from_ref, to_ref, held, arrived, left):
    size = to_ref.shape[1]
    columns = pl.ds(pl.multiple_of(rep[0] * size, HEAD_WIDTH), size)
    pieces = [pl.ds(n * BLOCK_TOKENS, BLOCK_TOKENS) for n in range(to_ref.shape[0] // BLOCK_TOKENS)]
    incoming = [
        pltpu.make_async_copy(from_ref.at[piece, columns], held.at[piece], arrived.at[n])
        for n, piece in enumerate(pieces)
    ]
    outgoing = [
        pltpu.make_async_copy(held.at[piece], to_ref.at[piece], left.at[n])
        for n, piece in enumerate(pieces)
    ]
    for copy in incoming:
        copy.start()
    for copy, onward in zip(incoming, outgoing):
        copy.wait()
        onward.start()
    for copy in outgoing:
        copy.wait()


def columns_kept(value, rep, size):
    rows = value.shape[0]
    pieces = rows // BLOCK_TOKENS
    return pl.pallas_call(
        kept_kernel,
        in_specs=[pl.BlockSpec(memory_space=pltpu.SMEM), pl.BlockSpec(memory_space=pl.ANY)],
        out_specs=pl.BlockSpec(memory_space=pl.ANY),
        out_shape=jax.ShapeDtypeStruct((rows, size), value.dtype),
        scratch_shapes=[
            pltpu.VMEM((rows, size), value.dtype),
            pltpu.SemaphoreType.DMA((pieces,)),
            pltpu.SemaphoreType.DMA((pieces,)),
        ],
        cost_estimate=pl.CostEstimate(
            flops=0, transcendentals=0, bytes_accessed=rows * size * 4
        ),
        name="columns_kept",
    )(rep.reshape(1), value)


def piece_starts(blocks):
    return [0, blocks - (blocks + 3) // 4]


def ring_order(count):
    return list(range(0, count, 2)) + list(range(count - 1, 0, -2))


def compacted(mask, columns, spare):
    place = jnp.cumsum(mask.astype(jnp.int32), axis=1) - 1
    slot = jnp.arange(mask.shape[1])
    chosen = mask[:, :, None] & (place[:, :, None] == slot[None, None, :])
    filled = jnp.sum(jnp.where(chosen[:, None], columns[None, :, :, None], 0), axis=2)
    counts = jnp.sum(mask.astype(jnp.int32), axis=1)
    empty = (slot[None, :] >= counts[:, None])[:, None, :]
    return jnp.where(empty, spare[None, :, None], filled), counts


def body(queries, prefill_keys, prefill_values, context_keys, context_values, picks):
    local_count, _, full_width = queries.shape
    rep_size = lax.axis_size("rep")
    ctx_size = lax.axis_size("ctx")
    rep_index = lax.axis_index("rep")
    ctx_index = lax.axis_index("ctx")
    width = full_width // rep_size
    key_width = prefill_keys.shape[2] // rep_size
    heads = width // HEAD_WIDTH
    head_grouping = width // key_width
    blocks_here = context_keys.shape[0] // BLOCK_TOKENS
    items = 2 * local_count * heads
    swap = [(0, 1), (1, 0)]

    def columns_of(value, which, size):
        return lax.dynamic_slice_in_dim(value, which * size, size, axis=value.ndim - 1)

    own_shard = (
        columns_kept(context_keys, rep_index, key_width),
        columns_kept(context_values, rep_index, key_width),
    )
    order = ring_order(ctx_size)
    onward = [(order[n], order[(n + 1) % ctx_size]) for n in range(ctx_size)]
    backward = [(target, source) for source, target in onward]

    def hop(value, pairs):
        return lax.ppermute(value, "ctx", pairs)

    shards = {0: own_shard}
    ahead, behind = own_shard, own_shard
    full_steps = (ctx_size - 1) // 2
    for step in range(1, full_steps):
        ahead = (hop(ahead[0], onward), hop(ahead[1], onward))
        behind = (hop(behind[0], backward), hop(behind[1], backward))
        shards[-step], shards[step] = ahead, behind
    starts = piece_starts(blocks_here)
    cut = starts[1] * BLOCK_TOKENS

    def hop_in_parts(shard, pairs):
        keys, values = shard
        return [
            (hop(keys[:cut], pairs), hop(values[:cut], pairs)),
            (hop(keys[cut:], pairs), hop(values[cut:], pairs)),
        ]

    ahead, behind = hop_in_parts(ahead, onward), hop_in_parts(behind, backward)
    step = full_steps + 1
    last_pieces = [
        (hop(keys, onward), hop(values, backward))
        for (keys, _), (_, values) in zip(ahead, behind)
    ]

    other = rep_size - 1 - rep_index

    def all_rows(value, size):
        kept = columns_of(value, rep_index, size)
        came = lax.ppermute(columns_of(value, other, size), "rep", swap)
        return jnp.where(
            rep_index == 0,
            jnp.concatenate([kept, came], axis=1),
            jnp.concatenate([came, kept], axis=1),
        )

    block_queries = all_rows(queries, width)
    block_keys = all_rows(prefill_keys, key_width)
    block_values = all_rows(prefill_values, key_width)

    position_of = [0] * ctx_size
    for position, device in enumerate(order):
        position_of[device] = position
    here = jnp.array(position_of, jnp.int32)[ctx_index]
    distances = sorted(shards, key=abs)
    late_distances = [-full_steps, full_steps, ctx_size // 2]
    wanted = jnp.array(order, jnp.int32)[
        (here + jnp.array(distances + late_distances, jnp.int32)) % ctx_size
    ]
    mine = lax.dynamic_slice_in_dim(picks[:, :, :2], rep_index * heads, heads, axis=1).reshape(-1)
    place = jnp.arange(items)
    head = place // 2 % heads
    holders = mine // blocks_here
    tile = mine - holders * blocks_here
    facts = [head // head_grouping, place // (2 * heads), head]
    tables, counts = compacted(
        holders[None, :] == wanted[:-3, None],
        jnp.stack([place, tile, *facts]),
        jnp.zeros((5,), jnp.int32),
    )
    first_tiles = jnp.array(starts, jnp.int32)
    piece_of = jnp.sum(tile[:, None] >= first_tiles[None, 1:], axis=1)
    halfway = holders == wanted[-1]
    reached = jnp.where(halfway, piece_of, jnp.minimum(piece_of, 1))
    piece_start = jnp.sum(
        jnp.where(reached[:, None] == jnp.arange(len(starts))[None, :], first_tiles[None, :], 0),
        axis=1,
    )
    sides = holders[None, :] == wanted[-3:-1, None]
    inside = jnp.concatenate(
        [
            sides & (reached == 0)[None, :],
            sides & (reached == 1)[None, :],
            halfway[None, :] & (piece_of[None, :] == jnp.arange(len(starts))[:, None]),
        ]
    )
    both = jnp.any(jnp.all(inside.reshape(4 + len(starts), -1, 2), axis=2), axis=0)
    both = jnp.stack([both, both], axis=1).reshape(-1)
    last_tables, last_counts = compacted(
        inside,
        jnp.stack(
            [
                place,
                tile - piece_start,
                *facts,
                jnp.where(both, items, place + 1 - 2 * (place % 2)),
                jnp.where(both, place % 2, 0),
            ]
        ),
        jnp.zeros((7,), jnp.int32),
    )
    ready, ready_counts = compacted(
        ~jnp.any(inside.reshape(1, -1, items // 2, 2), axis=(1, 3)),
        jnp.arange(items // 2)[None],
        jnp.zeros((1,), jnp.int32),
    )

    own, own_log, parts, logs, keep, send = own_attention(
        block_queries, block_keys, block_values, head_grouping, full_width
    )
    for n, distance in enumerate(distances):
        keys, values = shards[distance]
        parts, logs = pick_attention(n, tables, counts, block_queries, keys, values, parts, logs)
    keep, send = merge(
        rep_index, ready[0, 0], ready_counts[0], own, own_log, parts, logs, keep, send
    )
    state = (parts, logs, keep, send)
    late_arrivals = [list(pair) for pair in zip(ahead, behind)] + [[pair] for pair in last_pieces]
    row = 0
    for n, arrivals in enumerate(late_arrivals):
        state = final_attention(
            row,
            n + 1 < len(late_arrivals),
            rep_index,
            last_tables,
            last_counts,
            block_queries,
            arrivals,
            own,
            own_log,
            state,
        )
        row += len(arrivals)
    arriving = lax.ppermute(state[3], "rep", swap)
    return lax.dynamic_update_slice_in_dim(state[2], arriving, other * width, axis=2)


def solution(mesh):
    return jax.shard_map(
        body,
        mesh=mesh,
        in_specs=(
            P(("groups", "ctx"), "rep", "head"),
            P(("groups", "ctx"), "rep", "head"),
            P(("groups", "ctx"), "rep", "head"),
            P(("groups", "ctx"), "head"),
            P(("groups", "ctx"), "head"),
            P(("groups", "ctx"), "head", None),
        ),
        out_specs=P(("groups", "ctx"), "rep", "head"),
        check_vma=False,
    )
```

```python
import functools

import jax
import jax.numpy as jnp
from jax import lax
from jax.experimental import pallas as pl
from jax.experimental.pallas import tpu as pltpu
from jax.sharding import PartitionSpec as P


HEAD_WIDTH = 128
BLOCK_TOKENS = 512
SCALE = HEAD_WIDTH ** (-0.5)
LOG2E = 1.4426950408889634
NEGATIVE = -1e30


def fetched(shape, index_map):
    return pl.BlockSpec(shape, index_map, pipeline_mode=pl.Buffered(3))


def scores_by_key(keys, queries):
    return lax.dot_general(
        keys, queries, (((1,), (1,)), ((), ())), preferred_element_type=jnp.float32
    )


def mix_by_width(values, weights):
    return lax.dot_general(
        values,
        weights.astype(jnp.bfloat16),
        (((0,), (0,)), ((), ())),
        preferred_element_type=jnp.float32,
    )


def own_kernel(q_ref, k_ref, v_ref, part_ref, log_ref, *unwritten):
    half = q_ref.shape[1] // 2
    visible = lax.broadcasted_iota(jnp.int32, (half, half), 0) <= lax.broadcasted_iota(
        jnp.int32, (half, half), 1
    )
    early_keys, late_keys = k_ref[0, :half], k_ref[0, half:]
    early_queries, late_queries = q_ref[0, :half], q_ref[0, half:]

    first = jnp.where(visible, scores_by_key(early_keys, early_queries), NEGATIVE)
    highest = jnp.max(first, axis=0, keepdims=True)
    weights = jnp.exp2((first - highest) * (SCALE * LOG2E))
    total = jnp.sum(weights, axis=0, keepdims=True)
    part_ref[0, :, :half] = (mix_by_width(v_ref[0, :half], weights) / total).astype(
        part_ref.dtype
    )
    log_ref[0, :, :half] = highest * SCALE + jnp.log(total)

    before = scores_by_key(early_keys, late_queries)
    within = jnp.where(visible, scores_by_key(late_keys, late_queries), NEGATIVE)
    highest = jnp.maximum(
        jnp.max(before, axis=0, keepdims=True), jnp.max(within, axis=0, keepdims=True)
    )
    before = jnp.exp2((before - highest) * (SCALE * LOG2E))
    within = jnp.exp2((within - highest) * (SCALE * LOG2E))
    total = jnp.sum(before, axis=0, keepdims=True) + jnp.sum(within, axis=0, keepdims=True)
    mixed = mix_by_width(v_ref[0, :half], before) + mix_by_width(v_ref[0, half:], within)
    part_ref[0, :, half:] = (mixed / total).astype(part_ref.dtype)
    log_ref[0, :, half:] = highest * SCALE + jnp.log(total)


def own_attention(queries, keys, values, head_grouping, full_width):
    blocks, rows, width = queries.shape
    heads = width // HEAD_WIDTH
    count = blocks * heads
    items = 2 * count
    query_spec = pl.BlockSpec((1, rows, HEAD_WIDTH), lambda n: (lax.div(n, heads), 0, lax.rem(n, heads)))
    key_spec = pl.BlockSpec(
        (1, rows, HEAD_WIDTH), lambda n: (lax.div(n, heads), 0, lax.div(lax.rem(n, heads), head_grouping))
    )
    return pl.pallas_call(
        own_kernel,
        grid=(count,),
        in_specs=[query_spec, key_spec, key_spec],
        out_specs=[
            pl.BlockSpec((1, HEAD_WIDTH, rows), lambda n: (n, 0, 0)),
            pl.BlockSpec((1, 1, rows), lambda n: (n, 0, 0)),
        ]
        + [pl.BlockSpec(memory_space=pl.ANY)] * 4,
        out_shape=[
            jax.ShapeDtypeStruct((count, HEAD_WIDTH, rows), jnp.bfloat16),
            jax.ShapeDtypeStruct((count, 1, rows), jnp.float32),
            jax.ShapeDtypeStruct((items + 2, HEAD_WIDTH, rows), jnp.bfloat16),
            jax.ShapeDtypeStruct((items + 2, 1, rows), jnp.float32),
            jax.ShapeDtypeStruct((blocks, rows // 2, full_width), jnp.bfloat16),
            jax.ShapeDtypeStruct((blocks, rows // 2, width), jnp.bfloat16),
        ],
        cost_estimate=pl.CostEstimate(
            flops=count * rows * rows * HEAD_WIDTH * 4,
            transcendentals=count * rows * rows,
            bytes_accessed=count * rows * HEAD_WIDTH * 8,
        ),
        name="own_attention",
    )(queries, keys, values)


def attend_tile(queries, keys, values):
    scores = scores_by_key(keys, queries)
    highest = jnp.max(scores, axis=0, keepdims=True)
    weights = jnp.exp2((scores - highest) * (SCALE * LOG2E))
    total = jnp.sum(weights, axis=0, keepdims=True)
    part = (mix_by_width(values, weights) / total).astype(jnp.bfloat16)
    return part, highest * SCALE + jnp.log(total)


def when_any(count, pipeline, *arrays):
    @pl.when(count > 0)
    def _():
        pipeline(*arrays)


def pick_kernel(row, table, count, q_hbm, k_hbm, v_hbm, part_in, log_in, part_hbm, log_hbm):
    rows = q_hbm.shape[1]

    def attend(q_ref, k_ref, v_ref, part_ref, log_ref):
        part_ref[0], log_ref[0] = attend_tile(q_ref[0], k_ref[...], v_ref[...])

    tile = fetched((BLOCK_TOKENS, HEAD_WIDTH), lambda n: (table[row, 1, n], table[row, 2, n]))
    pipeline = pltpu.emit_pipeline(
        attend,
        grid=(count[row],),
        in_specs=[
            fetched((1, rows, HEAD_WIDTH), lambda n: (table[row, 3, n], 0, table[row, 4, n])),
            tile,
            tile,
        ],
        out_specs=[
            pl.BlockSpec((1, HEAD_WIDTH, rows), lambda n: (table[row, 0, n], 0, 0)),
            pl.BlockSpec((1, 1, rows), lambda n: (table[row, 0, n], 0, 0)),
        ],
    )
    when_any(count[row], pipeline, q_hbm, k_hbm, v_hbm, part_hbm, log_hbm)


def pick_attention(row, table, count, queries, keys, values, parts, logs):
    blocks, rows, width = queries.shape
    expected = 2 * blocks * (width // HEAD_WIDTH) // 8
    smem = pl.BlockSpec(memory_space=pltpu.SMEM)
    anywhere = pl.BlockSpec(memory_space=pl.ANY)
    return pl.pallas_call(
        functools.partial(pick_kernel, row),
        in_specs=[smem, smem] + [anywhere] * 5,
        out_specs=[anywhere, anywhere],
        out_shape=[
            jax.ShapeDtypeStruct(parts.shape, parts.dtype),
            jax.ShapeDtypeStruct(logs.shape, logs.dtype),
        ],
        input_output_aliases={5: 0, 6: 1},
        cost_estimate=pl.CostEstimate(
            flops=expected * rows * BLOCK_TOKENS * HEAD_WIDTH * 4,
            transcendentals=expected * rows * BLOCK_TOKENS,
            bytes_accessed=expected * rows * HEAD_WIDTH * 8,
        ),
        name="pick_attention",
    )(table, count, queries, keys, values, parts, logs)


def merged_rows(rep, own, own_log, first, first_log, second, second_log):
    half = own.shape[1] // 2
    top = jnp.maximum(own_log, jnp.maximum(first_log, second_log))
    own_share = jnp.exp(own_log - top)
    first_share = jnp.exp(first_log - top)
    second_share = jnp.exp(second_log - top)
    merged = (
        own_share * own.astype(jnp.float32)
        + first_share * first.astype(jnp.float32)
        + second_share * second.astype(jnp.float32)
    ) / (own_share + first_share + second_share)
    early = merged[:, :half].astype(jnp.bfloat16).T
    late = merged[:, half:].astype(jnp.bfloat16).T
    return jnp.where(rep == 0, early, late), jnp.where(rep == 0, late, early)


def merge_kernel(
    rep, ready, count, own_hbm, own_log_hbm, part_hbm, log_hbm, keep_in, send_in, keep_hbm, send_hbm
):
    rows = own_hbm.shape[2]
    half = rows // 2
    heads = send_hbm.shape[2] // HEAD_WIDTH

    def combine(own_ref, own_log_ref, part_ref, log_ref, keep_ref, send_ref):
        keep_ref[0], send_ref[0] = merged_rows(
            rep[0], own_ref[0], own_log_ref[0], part_ref[0], log_ref[0], part_ref[1], log_ref[1]
        )

    def place(n):
        return lax.div(ready[n], heads), lax.rem(ready[n], heads)

    pipeline = pltpu.emit_pipeline(
        combine,
        grid=(count[0],),
        in_specs=[
            fetched((1, HEAD_WIDTH, rows), lambda n: (ready[n], 0, 0)),
            fetched((1, 1, rows), lambda n: (ready[n], 0, 0)),
            fetched((2, HEAD_WIDTH, rows), lambda n: (ready[n], 0, 0)),
            fetched((2, 1, rows), lambda n: (ready[n], 0, 0)),
        ],
        out_specs=[
            pl.BlockSpec(
                (1, half, HEAD_WIDTH), lambda n: (place(n)[0], 0, rep[0] * heads + place(n)[1])
            ),
            pl.BlockSpec((1, half, HEAD_WIDTH), lambda n: (place(n)[0], 0, place(n)[1])),
        ],
    )
    when_any(count[0], pipeline, own_hbm, own_log_hbm, part_hbm, log_hbm, keep_hbm, send_hbm)


def merge(rep, ready, count, own, own_log, parts, logs, keep, send):
    heads, _, rows = own.shape
    smem = pl.BlockSpec(memory_space=pltpu.SMEM)
    anywhere = pl.BlockSpec(memory_space=pl.ANY)
    return pl.pallas_call(
        merge_kernel,
        in_specs=[smem] * 3 + [anywhere] * 6,
        out_specs=[anywhere, anywhere],
        out_shape=[
            jax.ShapeDtypeStruct(keep.shape, keep.dtype),
            jax.ShapeDtypeStruct(send.shape, send.dtype),
        ],
        input_output_aliases={7: 0, 8: 1},
        cost_estimate=pl.CostEstimate(
            flops=heads * rows * HEAD_WIDTH * 8,
            transcendentals=heads * rows * 3,
            bytes_accessed=heads * rows * HEAD_WIDTH * 10,
        ),
        name="merge_parts",
    )(rep.reshape(1), ready, count.reshape(1), own, own_log, parts, logs, keep, send)


def final_kernel(first_row, groups, keeps_parts, rep, table, count, q_hbm, *refs):
    arrivals, refs = refs[: 2 * groups], refs[2 * groups :]
    own_hbm, own_log_hbm, _, _, _, _, part_hbm, log_hbm, keep_hbm, send_hbm = refs[:10]
    step, held, held_log = refs[10:]
    rows = q_hbm.shape[1]
    half = rows // 2
    heads = send_hbm.shape[2] // HEAD_WIDTH
    wide = (1, HEAD_WIDTH, rows)

    def run(row, k_hbm, v_hbm):
        def attend(
            q_ref,
            k_ref,
            v_ref,
            own_ref,
            own_log_ref,
            other_ref,
            other_log_ref,
            keep_ref,
            send_ref,
            *part_refs,
        ):
            part, log = attend_tile(q_ref[0], k_ref[...], v_ref[...])
            second = table[row, 6, step[0]] == 1
            other = jnp.where(second, held[...], other_ref[0])
            other_log = jnp.where(second, held_log[...], other_log_ref[0])
            keep_ref[0], send_ref[0] = merged_rows(
                rep[0], own_ref[0], own_log_ref[0], part, log, other, other_log
            )
            if keeps_parts:
                part_refs[0][0], part_refs[1][0] = part, log
            held[...], held_log[...] = part, log
            step[0] += 1

        def at(column):
            return lambda n: (table[row, column, n], 0, 0)

        def own_at(n):
            return (table[row, 3, n] * heads + table[row, 4, n], 0, 0)

        tile = fetched(
            (BLOCK_TOKENS, HEAD_WIDTH), lambda n: (table[row, 1, n], table[row, 2, n])
        )
        step[0] = 0
        pipeline = pltpu.emit_pipeline(
            attend,
            grid=(count[row],),
            in_specs=[
                fetched(
                    (1, rows, HEAD_WIDTH), lambda n: (table[row, 3, n], 0, table[row, 4, n])
                ),
                tile,
                tile,
                fetched(wide, own_at),
                fetched((1, 1, rows), own_at),
                fetched(wide, at(5)),
                fetched((1, 1, rows), at(5)),
            ],
            out_specs=[
                pl.BlockSpec(
                    (1, half, HEAD_WIDTH),
                    lambda n: (table[row, 3, n], 0, rep[0] * heads + table[row, 4, n]),
                ),
                pl.BlockSpec(
                    (1, half, HEAD_WIDTH), lambda n: (table[row, 3, n], 0, table[row, 4, n])
                ),
                pl.BlockSpec(wide, at(0)),
                pl.BlockSpec((1, 1, rows), at(0)),
            ][: 4 if keeps_parts else 2],
        )
        when_any(
            count[row],
            pipeline,
            q_hbm,
            k_hbm,
            v_hbm,
            own_hbm,
            own_log_hbm,
            part_hbm,
            log_hbm,
            *(keep_hbm, send_hbm, part_hbm, log_hbm)[: 4 if keeps_parts else 2],
        )

    for n in range(groups):
        run(first_row + n, arrivals[2 * n], arrivals[2 * n + 1])


def final_attention(first_row, keeps_parts, rep, table, count, queries, arrivals, own, own_log, state):
    rows = queries.shape[1]
    groups = len(arrivals)
    expected = own.shape[0] * groups // 8
    smem = pl.BlockSpec(memory_space=pltpu.SMEM)
    anywhere = pl.BlockSpec(memory_space=pl.ANY)
    flat = [array for pair in arrivals for array in pair]
    return pl.pallas_call(
        functools.partial(final_kernel, first_row, groups, keeps_parts),
        in_specs=[smem] * 3 + [anywhere] * (7 + len(flat)),
        out_specs=[anywhere] * 4,
        out_shape=[jax.ShapeDtypeStruct(value.shape, value.dtype) for value in state],
        scratch_shapes=[
            pltpu.SMEM((1,), jnp.int32),
            pltpu.VMEM((HEAD_WIDTH, rows), jnp.bfloat16),
            pltpu.VMEM((1, rows), jnp.float32),
        ],
        input_output_aliases={6 + len(flat) + n: n for n in range(4)},
        cost_estimate=pl.CostEstimate(
            flops=expected * rows * BLOCK_TOKENS * HEAD_WIDTH * 4,
            transcendentals=expected * rows * BLOCK_TOKENS,
            bytes_accessed=expected * rows * HEAD_WIDTH * 18,
        ),
        name="final_attention",
    )(rep.reshape(1), table, count, queries, *flat, own, own_log, *state)


def kept_kernel(rep, from_ref, to_ref, held, arrived, left):
    size = to_ref.shape[1]
    columns = pl.ds(pl.multiple_of(rep[0] * size, HEAD_WIDTH), size)
    pieces = [pl.ds(n * BLOCK_TOKENS, BLOCK_TOKENS) for n in range(to_ref.shape[0] // BLOCK_TOKENS)]
    incoming = [
        pltpu.make_async_copy(from_ref.at[piece, columns], held.at[piece], arrived.at[n])
        for n, piece in enumerate(pieces)
    ]
    outgoing = [
        pltpu.make_async_copy(held.at[piece], to_ref.at[piece], left.at[n])
        for n, piece in enumerate(pieces)
    ]
    for copy in incoming:
        copy.start()
    for copy, onward in zip(incoming, outgoing):
        copy.wait()
        onward.start()
    for copy in outgoing:
        copy.wait()


def columns_kept(value, rep, size):
    rows = value.shape[0]
    pieces = rows // BLOCK_TOKENS
    return pl.pallas_call(
        kept_kernel,
        in_specs=[pl.BlockSpec(memory_space=pltpu.SMEM), pl.BlockSpec(memory_space=pl.ANY)],
        out_specs=pl.BlockSpec(memory_space=pl.ANY),
        out_shape=jax.ShapeDtypeStruct((rows, size), value.dtype),
        scratch_shapes=[
            pltpu.VMEM((rows, size), value.dtype),
            pltpu.SemaphoreType.DMA((pieces,)),
            pltpu.SemaphoreType.DMA((pieces,)),
        ],
        cost_estimate=pl.CostEstimate(
            flops=0, transcendentals=0, bytes_accessed=rows * size * 4
        ),
        name="columns_kept",
    )(rep.reshape(1), value)


def piece_starts(blocks):
    return [0, (blocks + 1) // 2]


def ring_order(count):
    return list(range(0, count, 2)) + list(range(count - 1, 0, -2))


def compacted(mask, columns, spare):
    place = jnp.cumsum(mask.astype(jnp.int32), axis=1) - 1
    slot = jnp.arange(mask.shape[1])
    chosen = mask[:, :, None] & (place[:, :, None] == slot[None, None, :])
    filled = jnp.sum(jnp.where(chosen[:, None], columns[None, :, :, None], 0), axis=2)
    counts = jnp.sum(mask.astype(jnp.int32), axis=1)
    empty = (slot[None, :] >= counts[:, None])[:, None, :]
    return jnp.where(empty, spare[None, :, None], filled), counts


def body(queries, prefill_keys, prefill_values, context_keys, context_values, picks):
    local_count, _, full_width = queries.shape
    rep_size = lax.axis_size("rep")
    ctx_size = lax.axis_size("ctx")
    rep_index = lax.axis_index("rep")
    ctx_index = lax.axis_index("ctx")
    width = full_width // rep_size
    key_width = prefill_keys.shape[2] // rep_size
    heads = width // HEAD_WIDTH
    head_grouping = width // key_width
    blocks_here = context_keys.shape[0] // BLOCK_TOKENS
    items = 2 * local_count * heads
    swap = [(0, 1), (1, 0)]

    def columns_of(value, which, size):
        return lax.dynamic_slice_in_dim(value, which * size, size, axis=value.ndim - 1)

    own_shard = (
        columns_kept(context_keys, rep_index, key_width),
        columns_kept(context_values, rep_index, key_width),
    )
    order = ring_order(ctx_size)
    onward = [(order[n], order[(n + 1) % ctx_size]) for n in range(ctx_size)]
    backward = [(target, source) for source, target in onward]

    def hop(value, pairs):
        return lax.ppermute(value, "ctx", pairs)

    shards = {0: own_shard}
    ahead, behind = own_shard, own_shard
    full_steps = (ctx_size - 1) // 2
    for step in range(1, full_steps):
        ahead = (hop(ahead[0], onward), hop(ahead[1], onward))
        behind = (hop(behind[0], backward), hop(behind[1], backward))
        shards[-step], shards[step] = ahead, behind
    starts = piece_starts(blocks_here)
    cut = starts[1] * BLOCK_TOKENS

    def hop_in_parts(shard, pairs):
        keys, values = shard
        return [
            (hop(keys[:cut], pairs), hop(values[:cut], pairs)),
            (hop(keys[cut:], pairs), hop(values[cut:], pairs)),
        ]

    ahead, behind = hop_in_parts(ahead, onward), hop_in_parts(behind, backward)
    step = full_steps + 1
    last_pieces = [
        (hop(keys, onward), hop(values, backward))
        for (keys, _), (_, values) in zip(ahead, behind)
    ]

    other = rep_size - 1 - rep_index

    def all_rows(value, size):
        kept = columns_of(value, rep_index, size)
        came = lax.ppermute(columns_of(value, other, size), "rep", swap)
        return jnp.where(
            rep_index == 0,
            jnp.concatenate([kept, came], axis=1),
            jnp.concatenate([came, kept], axis=1),
        )

    block_queries = all_rows(queries, width)
    block_keys = all_rows(prefill_keys, key_width)
    block_values = all_rows(prefill_values, key_width)

    position_of = [0] * ctx_size
    for position, device in enumerate(order):
        position_of[device] = position
    here = jnp.array(position_of, jnp.int32)[ctx_index]
    distances = sorted(shards, key=abs)
    late_distances = [-full_steps, full_steps, ctx_size // 2]
    wanted = jnp.array(order, jnp.int32)[
        (here + jnp.array(distances + late_distances, jnp.int32)) % ctx_size
    ]
    mine = lax.dynamic_slice_in_dim(picks[:, :, :2], rep_index * heads, heads, axis=1).reshape(-1)
    place = jnp.arange(items)
    head = place // 2 % heads
    holders = mine // blocks_here
    tile = mine - holders * blocks_here
    facts = [head // head_grouping, place // (2 * heads), head]
    tables, counts = compacted(
        holders[None, :] == wanted[:-3, None],
        jnp.stack([place, tile, *facts]),
        jnp.zeros((5,), jnp.int32),
    )
    first_tiles = jnp.array(starts, jnp.int32)
    piece_of = jnp.sum(tile[:, None] >= first_tiles[None, 1:], axis=1)
    halfway = holders == wanted[-1]
    reached = jnp.where(halfway, piece_of, jnp.minimum(piece_of, 1))
    piece_start = jnp.sum(
        jnp.where(reached[:, None] == jnp.arange(len(starts))[None, :], first_tiles[None, :], 0),
        axis=1,
    )
    sides = holders[None, :] == wanted[-3:-1, None]
    inside = jnp.concatenate(
        [
            sides & (reached == 0)[None, :],
            sides & (reached == 1)[None, :],
            halfway[None, :] & (piece_of[None, :] == jnp.arange(len(starts))[:, None]),
        ]
    )
    both = jnp.any(jnp.all(inside.reshape(4 + len(starts), -1, 2), axis=2), axis=0)
    both = jnp.stack([both, both], axis=1).reshape(-1)
    last_tables, last_counts = compacted(
        inside,
        jnp.stack(
            [
                place,
                tile - piece_start,
                *facts,
                jnp.where(both, items, place + 1 - 2 * (place % 2)),
                jnp.where(both, place % 2, 0),
            ]
        ),
        jnp.zeros((7,), jnp.int32),
    )
    ready, ready_counts = compacted(
        ~jnp.any(inside.reshape(1, -1, items // 2, 2), axis=(1, 3)),
        jnp.arange(items // 2)[None],
        jnp.zeros((1,), jnp.int32),
    )

    own, own_log, parts, logs, keep, send = own_attention(
        block_queries, block_keys, block_values, head_grouping, full_width
    )
    for n, distance in enumerate(distances):
        keys, values = shards[distance]
        parts, logs = pick_attention(n, tables, counts, block_queries, keys, values, parts, logs)
    keep, send = merge(
        rep_index, ready[0, 0], ready_counts[0], own, own_log, parts, logs, keep, send
    )
    state = (parts, logs, keep, send)
    late_arrivals = [list(pair) for pair in zip(ahead, behind)] + [[pair] for pair in last_pieces]
    row = 0
    for n, arrivals in enumerate(late_arrivals):
        state = final_attention(
            row,
            n + 1 < len(late_arrivals),
            rep_index,
            last_tables,
            last_counts,
            block_queries,
            arrivals,
            own,
            own_log,
            state,
        )
        row += len(arrivals)
    arriving = lax.ppermute(state[3], "rep", swap)
    return lax.dynamic_update_slice_in_dim(state[2], arriving, other * width, axis=2)


def solution(mesh):
    return jax.shard_map(
        body,
        mesh=mesh,
        in_specs=(
            P(("groups", "ctx"), "rep", "head"),
            P(("groups", "ctx"), "rep", "head"),
            P(("groups", "ctx"), "rep", "head"),
            P(("groups", "ctx"), "head"),
            P(("groups", "ctx"), "head"),
            P(("groups", "ctx"), "head", None),
        ),
        out_specs=P(("groups", "ctx"), "rep", "head"),
        check_vma=False,
    )
```

```python
import functools

import jax
import jax.numpy as jnp
from jax import lax
from jax.experimental import pallas as pl
from jax.experimental.pallas import tpu as pltpu
from jax.sharding import PartitionSpec as P


HEAD_WIDTH = 128
BLOCK_TOKENS = 512
SCALE = HEAD_WIDTH ** (-0.5)
LOG2E = 1.4426950408889634
NEGATIVE = -1e30


def fetched(shape, index_map):
    return pl.BlockSpec(shape, index_map, pipeline_mode=pl.Buffered(3))


def scores_by_key(keys, queries):
    return lax.dot_general(
        keys, queries, (((1,), (1,)), ((), ())), preferred_element_type=jnp.float32
    )


def mix_by_width(values, weights):
    return lax.dot_general(
        values,
        weights.astype(jnp.bfloat16),
        (((0,), (0,)), ((), ())),
        preferred_element_type=jnp.float32,
    )


def own_kernel(q_ref, k_ref, v_ref, part_ref, log_ref, *unwritten):
    half = q_ref.shape[1] // 2
    visible = lax.broadcasted_iota(jnp.int32, (half, half), 0) <= lax.broadcasted_iota(
        jnp.int32, (half, half), 1
    )
    early_keys, late_keys = k_ref[0, :half], k_ref[0, half:]
    early_queries, late_queries = q_ref[0, :half], q_ref[0, half:]

    first = jnp.where(visible, scores_by_key(early_keys, early_queries), NEGATIVE)
    highest = jnp.max(first, axis=0, keepdims=True)
    weights = jnp.exp2((first - highest) * (SCALE * LOG2E))
    total = jnp.sum(weights, axis=0, keepdims=True)
    part_ref[0, :, :half] = (mix_by_width(v_ref[0, :half], weights) * (1.0 / total)).astype(
        part_ref.dtype
    )
    log_ref[0, :, :half] = highest * SCALE + jnp.log(total)

    before = scores_by_key(early_keys, late_queries)
    within = jnp.where(visible, scores_by_key(late_keys, late_queries), NEGATIVE)
    highest = jnp.maximum(
        jnp.max(before, axis=0, keepdims=True), jnp.max(within, axis=0, keepdims=True)
    )
    before = jnp.exp2((before - highest) * (SCALE * LOG2E))
    within = jnp.exp2((within - highest) * (SCALE * LOG2E))
    total = jnp.sum(before, axis=0, keepdims=True) + jnp.sum(within, axis=0, keepdims=True)
    mixed = mix_by_width(v_ref[0, :half], before) + mix_by_width(v_ref[0, half:], within)
    part_ref[0, :, half:] = (mixed * (1.0 / total)).astype(part_ref.dtype)
    log_ref[0, :, half:] = highest * SCALE + jnp.log(total)


def own_attention(queries, keys, values, head_grouping, full_width):
    blocks, rows, width = queries.shape
    heads = width // HEAD_WIDTH
    count = blocks * heads
    items = 2 * count
    query_spec = pl.BlockSpec((1, rows, HEAD_WIDTH), lambda n: (lax.div(n, heads), 0, lax.rem(n, heads)))
    key_spec = pl.BlockSpec(
        (1, rows, HEAD_WIDTH), lambda n: (lax.div(n, heads), 0, lax.div(lax.rem(n, heads), head_grouping))
    )
    return pl.pallas_call(
        own_kernel,
        grid=(count,),
        in_specs=[query_spec, key_spec, key_spec],
        out_specs=[
            pl.BlockSpec((1, HEAD_WIDTH, rows), lambda n: (n, 0, 0)),
            pl.BlockSpec((1, 1, rows), lambda n: (n, 0, 0)),
        ]
        + [pl.BlockSpec(memory_space=pl.ANY)] * 4,
        out_shape=[
            jax.ShapeDtypeStruct((count, HEAD_WIDTH, rows), jnp.bfloat16),
            jax.ShapeDtypeStruct((count, 1, rows), jnp.float32),
            jax.ShapeDtypeStruct((items + 2, HEAD_WIDTH, rows), jnp.bfloat16),
            jax.ShapeDtypeStruct((items + 2, 1, rows), jnp.float32),
            jax.ShapeDtypeStruct((blocks, rows // 2, full_width), jnp.bfloat16),
            jax.ShapeDtypeStruct((blocks, rows // 2, width), jnp.bfloat16),
        ],
        cost_estimate=pl.CostEstimate(
            flops=count * rows * rows * HEAD_WIDTH * 4,
            transcendentals=count * rows * rows,
            bytes_accessed=count * rows * HEAD_WIDTH * 8,
        ),
        name="own_attention",
    )(queries, keys, values)


def attend_tile(queries, keys, values):
    scores = scores_by_key(keys, queries)
    highest = jnp.max(scores, axis=0, keepdims=True)
    weights = jnp.exp2((scores - highest) * (SCALE * LOG2E))
    total = jnp.sum(weights, axis=0, keepdims=True)
    part = (mix_by_width(values, weights) * (1.0 / total)).astype(jnp.bfloat16)
    return part, highest * SCALE + jnp.log(total)


def when_any(count, pipeline, *arrays):
    @pl.when(count > 0)
    def _():
        pipeline(*arrays)


def pick_kernel(row, table, count, q_hbm, k_hbm, v_hbm, part_in, log_in, part_hbm, log_hbm):
    rows = q_hbm.shape[1]

    def attend(q_ref, k_ref, v_ref, part_ref, log_ref):
        part_ref[0], log_ref[0] = attend_tile(q_ref[0], k_ref[...], v_ref[...])

    tile = fetched((BLOCK_TOKENS, HEAD_WIDTH), lambda n: (table[row, 1, n], table[row, 2, n]))
    pipeline = pltpu.emit_pipeline(
        attend,
        grid=(count[row],),
        in_specs=[
            fetched((1, rows, HEAD_WIDTH), lambda n: (table[row, 3, n], 0, table[row, 4, n])),
            tile,
            tile,
        ],
        out_specs=[
            pl.BlockSpec((1, HEAD_WIDTH, rows), lambda n: (table[row, 0, n], 0, 0)),
            pl.BlockSpec((1, 1, rows), lambda n: (table[row, 0, n], 0, 0)),
        ],
    )
    when_any(count[row], pipeline, q_hbm, k_hbm, v_hbm, part_hbm, log_hbm)


def pick_attention(row, table, count, queries, keys, values, parts, logs):
    blocks, rows, width = queries.shape
    expected = 2 * blocks * (width // HEAD_WIDTH) // 8
    smem = pl.BlockSpec(memory_space=pltpu.SMEM)
    anywhere = pl.BlockSpec(memory_space=pl.ANY)
    return pl.pallas_call(
        functools.partial(pick_kernel, row),
        in_specs=[smem, smem] + [anywhere] * 5,
        out_specs=[anywhere, anywhere],
        out_shape=[
            jax.ShapeDtypeStruct(parts.shape, parts.dtype),
            jax.ShapeDtypeStruct(logs.shape, logs.dtype),
        ],
        input_output_aliases={5: 0, 6: 1},
        cost_estimate=pl.CostEstimate(
            flops=expected * rows * BLOCK_TOKENS * HEAD_WIDTH * 4,
            transcendentals=expected * rows * BLOCK_TOKENS,
            bytes_accessed=expected * rows * HEAD_WIDTH * 8,
        ),
        name="pick_attention",
    )(table, count, queries, keys, values, parts, logs)


def merged_rows(rep, own, own_log, first, first_log, second, second_log):
    half = own.shape[1] // 2
    top = jnp.maximum(own_log, jnp.maximum(first_log, second_log))
    own_share = jnp.exp(own_log - top)
    first_share = jnp.exp(first_log - top)
    second_share = jnp.exp(second_log - top)
    whole = 1.0 / (own_share + first_share + second_share)
    merged = (
        (own_share * whole) * own.astype(jnp.float32)
        + (first_share * whole) * first.astype(jnp.float32)
        + (second_share * whole) * second.astype(jnp.float32)
    )
    early = merged[:, :half].astype(jnp.bfloat16).T
    late = merged[:, half:].astype(jnp.bfloat16).T
    return jnp.where(rep == 0, early, late), jnp.where(rep == 0, late, early)


def merge_kernel(
    rep, ready, count, own_hbm, own_log_hbm, part_hbm, log_hbm, keep_in, send_in, keep_hbm, send_hbm
):
    rows = own_hbm.shape[2]
    half = rows // 2
    heads = send_hbm.shape[2] // HEAD_WIDTH

    def combine(own_ref, own_log_ref, part_ref, log_ref, keep_ref, send_ref):
        keep_ref[0], send_ref[0] = merged_rows(
            rep[0], own_ref[0], own_log_ref[0], part_ref[0], log_ref[0], part_ref[1], log_ref[1]
        )

    def place(n):
        return lax.div(ready[n], heads), lax.rem(ready[n], heads)

    pipeline = pltpu.emit_pipeline(
        combine,
        grid=(count[0],),
        in_specs=[
            fetched((1, HEAD_WIDTH, rows), lambda n: (ready[n], 0, 0)),
            fetched((1, 1, rows), lambda n: (ready[n], 0, 0)),
            fetched((2, HEAD_WIDTH, rows), lambda n: (ready[n], 0, 0)),
            fetched((2, 1, rows), lambda n: (ready[n], 0, 0)),
        ],
        out_specs=[
            pl.BlockSpec(
                (1, half, HEAD_WIDTH), lambda n: (place(n)[0], 0, rep[0] * heads + place(n)[1])
            ),
            pl.BlockSpec((1, half, HEAD_WIDTH), lambda n: (place(n)[0], 0, place(n)[1])),
        ],
    )
    when_any(count[0], pipeline, own_hbm, own_log_hbm, part_hbm, log_hbm, keep_hbm, send_hbm)


def merge(rep, ready, count, own, own_log, parts, logs, keep, send):
    heads, _, rows = own.shape
    smem = pl.BlockSpec(memory_space=pltpu.SMEM)
    anywhere = pl.BlockSpec(memory_space=pl.ANY)
    return pl.pallas_call(
        merge_kernel,
        in_specs=[smem] * 3 + [anywhere] * 6,
        out_specs=[anywhere, anywhere],
        out_shape=[
            jax.ShapeDtypeStruct(keep.shape, keep.dtype),
            jax.ShapeDtypeStruct(send.shape, send.dtype),
        ],
        input_output_aliases={7: 0, 8: 1},
        cost_estimate=pl.CostEstimate(
            flops=heads * rows * HEAD_WIDTH * 8,
            transcendentals=heads * rows * 3,
            bytes_accessed=heads * rows * HEAD_WIDTH * 10,
        ),
        name="merge_parts",
    )(rep.reshape(1), ready, count.reshape(1), own, own_log, parts, logs, keep, send)


def final_kernel(first_row, groups, keeps_parts, rep, table, count, q_hbm, *refs):
    arrivals, refs = refs[: 2 * groups], refs[2 * groups :]
    own_hbm, own_log_hbm, _, _, _, _, part_hbm, log_hbm, keep_hbm, send_hbm = refs[:10]
    step, held, held_log = refs[10:]
    rows = q_hbm.shape[1]
    half = rows // 2
    heads = send_hbm.shape[2] // HEAD_WIDTH
    wide = (1, HEAD_WIDTH, rows)

    def run(row, k_hbm, v_hbm):
        def attend(
            q_ref,
            k_ref,
            v_ref,
            own_ref,
            own_log_ref,
            other_ref,
            other_log_ref,
            keep_ref,
            send_ref,
            *part_refs,
        ):
            part, log = attend_tile(q_ref[0], k_ref[...], v_ref[...])
            second = table[row, 6, step[0]] == 1
            other = jnp.where(second, held[...], other_ref[0])
            other_log = jnp.where(second, held_log[...], other_log_ref[0])
            keep_ref[0], send_ref[0] = merged_rows(
                rep[0], own_ref[0], own_log_ref[0], part, log, other, other_log
            )
            if keeps_parts:
                part_refs[0][0], part_refs[1][0] = part, log
            held[...], held_log[...] = part, log
            step[0] += 1

        def at(column):
            return lambda n: (table[row, column, n], 0, 0)

        def own_at(n):
            return (table[row, 3, n] * heads + table[row, 4, n], 0, 0)

        tile = fetched(
            (BLOCK_TOKENS, HEAD_WIDTH), lambda n: (table[row, 1, n], table[row, 2, n])
        )
        step[0] = 0
        pipeline = pltpu.emit_pipeline(
            attend,
            grid=(count[row],),
            in_specs=[
                fetched(
                    (1, rows, HEAD_WIDTH), lambda n: (table[row, 3, n], 0, table[row, 4, n])
                ),
                tile,
                tile,
                fetched(wide, own_at),
                fetched((1, 1, rows), own_at),
                fetched(wide, at(5)),
                fetched((1, 1, rows), at(5)),
            ],
            out_specs=[
                pl.BlockSpec(
                    (1, half, HEAD_WIDTH),
                    lambda n: (table[row, 3, n], 0, rep[0] * heads + table[row, 4, n]),
                ),
                pl.BlockSpec(
                    (1, half, HEAD_WIDTH), lambda n: (table[row, 3, n], 0, table[row, 4, n])
                ),
                pl.BlockSpec(wide, at(0)),
                pl.BlockSpec((1, 1, rows), at(0)),
            ][: 4 if keeps_parts else 2],
        )
        when_any(
            count[row],
            pipeline,
            q_hbm,
            k_hbm,
            v_hbm,
            own_hbm,
            own_log_hbm,
            part_hbm,
            log_hbm,
            *(keep_hbm, send_hbm, part_hbm, log_hbm)[: 4 if keeps_parts else 2],
        )

    for n in range(groups):
        run(first_row + n, arrivals[2 * n], arrivals[2 * n + 1])


def final_attention(first_row, keeps_parts, rep, table, count, queries, arrivals, own, own_log, state):
    rows = queries.shape[1]
    groups = len(arrivals)
    expected = own.shape[0] * groups // 8
    smem = pl.BlockSpec(memory_space=pltpu.SMEM)
    anywhere = pl.BlockSpec(memory_space=pl.ANY)
    flat = [array for pair in arrivals for array in pair]
    return pl.pallas_call(
        functools.partial(final_kernel, first_row, groups, keeps_parts),
        in_specs=[smem] * 3 + [anywhere] * (7 + len(flat)),
        out_specs=[anywhere] * 4,
        out_shape=[jax.ShapeDtypeStruct(value.shape, value.dtype) for value in state],
        scratch_shapes=[
            pltpu.SMEM((1,), jnp.int32),
            pltpu.VMEM((HEAD_WIDTH, rows), jnp.bfloat16),
            pltpu.VMEM((1, rows), jnp.float32),
        ],
        input_output_aliases={6 + len(flat) + n: n for n in range(4)},
        cost_estimate=pl.CostEstimate(
            flops=expected * rows * BLOCK_TOKENS * HEAD_WIDTH * 4,
            transcendentals=expected * rows * BLOCK_TOKENS,
            bytes_accessed=expected * rows * HEAD_WIDTH * 18,
        ),
        name="final_attention",
    )(rep.reshape(1), table, count, queries, *flat, own, own_log, *state)


def kept_kernel(rep, from_ref, to_ref, held, arrived, left):
    size = to_ref.shape[1]
    columns = pl.ds(pl.multiple_of(rep[0] * size, HEAD_WIDTH), size)
    pieces = [pl.ds(n * BLOCK_TOKENS, BLOCK_TOKENS) for n in range(to_ref.shape[0] // BLOCK_TOKENS)]
    incoming = [
        pltpu.make_async_copy(from_ref.at[piece, columns], held.at[piece], arrived.at[n])
        for n, piece in enumerate(pieces)
    ]
    outgoing = [
        pltpu.make_async_copy(held.at[piece], to_ref.at[piece], left.at[n])
        for n, piece in enumerate(pieces)
    ]
    for copy in incoming:
        copy.start()
    for copy, onward in zip(incoming, outgoing):
        copy.wait()
        onward.start()
    for copy in outgoing:
        copy.wait()


def columns_kept(value, rep, size):
    rows = value.shape[0]
    pieces = rows // BLOCK_TOKENS
    return pl.pallas_call(
        kept_kernel,
        in_specs=[pl.BlockSpec(memory_space=pltpu.SMEM), pl.BlockSpec(memory_space=pl.ANY)],
        out_specs=pl.BlockSpec(memory_space=pl.ANY),
        out_shape=jax.ShapeDtypeStruct((rows, size), value.dtype),
        scratch_shapes=[
            pltpu.VMEM((rows, size), value.dtype),
            pltpu.SemaphoreType.DMA((pieces,)),
            pltpu.SemaphoreType.DMA((pieces,)),
        ],
        cost_estimate=pl.CostEstimate(
            flops=0, transcendentals=0, bytes_accessed=rows * size * 4
        ),
        name="columns_kept",
    )(rep.reshape(1), value)


def piece_starts(blocks):
    return [0, (blocks + 1) // 2]


def ring_order(count):
    return list(range(0, count, 2)) + list(range(count - 1, 0, -2))


def compacted(mask, columns, spare):
    place = jnp.cumsum(mask.astype(jnp.int32), axis=1) - 1
    slot = jnp.arange(mask.shape[1])
    chosen = mask[:, :, None] & (place[:, :, None] == slot[None, None, :])
    filled = jnp.sum(jnp.where(chosen[:, None], columns[None, :, :, None], 0), axis=2)
    counts = jnp.sum(mask.astype(jnp.int32), axis=1)
    empty = (slot[None, :] >= counts[:, None])[:, None, :]
    return jnp.where(empty, spare[None, :, None], filled), counts


def body(queries, prefill_keys, prefill_values, context_keys, context_values, picks):
    local_count, _, full_width = queries.shape
    rep_size = lax.axis_size("rep")
    ctx_size = lax.axis_size("ctx")
    rep_index = lax.axis_index("rep")
    ctx_index = lax.axis_index("ctx")
    width = full_width // rep_size
    key_width = prefill_keys.shape[2] // rep_size
    heads = width // HEAD_WIDTH
    head_grouping = width // key_width
    blocks_here = context_keys.shape[0] // BLOCK_TOKENS
    items = 2 * local_count * heads
    swap = [(0, 1), (1, 0)]

    def columns_of(value, which, size):
        return lax.dynamic_slice_in_dim(value, which * size, size, axis=value.ndim - 1)

    own_shard = (
        columns_kept(context_keys, rep_index, key_width),
        columns_kept(context_values, rep_index, key_width),
    )
    order = ring_order(ctx_size)
    onward = [(order[n], order[(n + 1) % ctx_size]) for n in range(ctx_size)]
    backward = [(target, source) for source, target in onward]

    def hop(value, pairs):
        return lax.ppermute(value, "ctx", pairs)

    shards = {0: own_shard}
    ahead, behind = own_shard, own_shard
    full_steps = (ctx_size - 1) // 2
    for step in range(1, full_steps):
        ahead = (hop(ahead[0], onward), hop(ahead[1], onward))
        behind = (hop(behind[0], backward), hop(behind[1], backward))
        shards[-step], shards[step] = ahead, behind
    starts = piece_starts(blocks_here)
    cut = starts[1] * BLOCK_TOKENS

    def hop_in_parts(shard, pairs):
        keys, values = shard
        return [
            (hop(keys[:cut], pairs), hop(values[:cut], pairs)),
            (hop(keys[cut:], pairs), hop(values[cut:], pairs)),
        ]

    ahead, behind = hop_in_parts(ahead, onward), hop_in_parts(behind, backward)
    step = full_steps + 1
    last_pieces = [
        (hop(keys, onward), hop(values, backward))
        for (keys, _), (_, values) in zip(ahead, behind)
    ]

    other = rep_size - 1 - rep_index

    def all_rows(value, size):
        kept = columns_of(value, rep_index, size)
        came = lax.ppermute(columns_of(value, other, size), "rep", swap)
        return jnp.where(
            rep_index == 0,
            jnp.concatenate([kept, came], axis=1),
            jnp.concatenate([came, kept], axis=1),
        )

    block_queries = all_rows(queries, width)
    block_keys = all_rows(prefill_keys, key_width)
    block_values = all_rows(prefill_values, key_width)

    position_of = [0] * ctx_size
    for position, device in enumerate(order):
        position_of[device] = position
    here = jnp.array(position_of, jnp.int32)[ctx_index]
    distances = sorted(shards, key=abs)
    late_distances = [-full_steps, full_steps, ctx_size // 2]
    wanted = jnp.array(order, jnp.int32)[
        (here + jnp.array(distances + late_distances, jnp.int32)) % ctx_size
    ]
    mine = lax.dynamic_slice_in_dim(picks[:, :, :2], rep_index * heads, heads, axis=1).reshape(-1)
    place = jnp.arange(items)
    head = place // 2 % heads
    holders = mine // blocks_here
    tile = mine - holders * blocks_here
    facts = [head // head_grouping, place // (2 * heads), head]
    tables, counts = compacted(
        holders[None, :] == wanted[:-3, None],
        jnp.stack([place, tile, *facts]),
        jnp.zeros((5,), jnp.int32),
    )
    first_tiles = jnp.array(starts, jnp.int32)
    piece_of = jnp.sum(tile[:, None] >= first_tiles[None, 1:], axis=1)
    halfway = holders == wanted[-1]
    reached = jnp.where(halfway, piece_of, jnp.minimum(piece_of, 1))
    piece_start = jnp.sum(
        jnp.where(reached[:, None] == jnp.arange(len(starts))[None, :], first_tiles[None, :], 0),
        axis=1,
    )
    sides = holders[None, :] == wanted[-3:-1, None]
    inside = jnp.concatenate(
        [
            sides & (reached == 0)[None, :],
            sides & (reached == 1)[None, :],
            halfway[None, :] & (piece_of[None, :] == jnp.arange(len(starts))[:, None]),
        ]
    )
    both = jnp.any(jnp.all(inside.reshape(4 + len(starts), -1, 2), axis=2), axis=0)
    both = jnp.stack([both, both], axis=1).reshape(-1)
    last_tables, last_counts = compacted(
        inside,
        jnp.stack(
            [
                place,
                tile - piece_start,
                *facts,
                jnp.where(both, items, place + 1 - 2 * (place % 2)),
                jnp.where(both, place % 2, 0),
            ]
        ),
        jnp.zeros((7,), jnp.int32),
    )
    ready, ready_counts = compacted(
        ~jnp.any(inside.reshape(1, -1, items // 2, 2), axis=(1, 3)),
        jnp.arange(items // 2)[None],
        jnp.zeros((1,), jnp.int32),
    )

    own, own_log, parts, logs, keep, send = own_attention(
        block_queries, block_keys, block_values, head_grouping, full_width
    )
    for n, distance in enumerate(distances):
        keys, values = shards[distance]
        parts, logs = pick_attention(n, tables, counts, block_queries, keys, values, parts, logs)
    keep, send = merge(
        rep_index, ready[0, 0], ready_counts[0], own, own_log, parts, logs, keep, send
    )
    state = (parts, logs, keep, send)
    late_arrivals = [list(pair) for pair in zip(ahead, behind)] + [[pair] for pair in last_pieces]
    row = 0
    for n, arrivals in enumerate(late_arrivals):
        state = final_attention(
            row,
            n + 1 < len(late_arrivals),
            rep_index,
            last_tables,
            last_counts,
            block_queries,
            arrivals,
            own,
            own_log,
            state,
        )
        row += len(arrivals)
    arriving = lax.ppermute(state[3], "rep", swap)
    return lax.dynamic_update_slice_in_dim(state[2], arriving, other * width, axis=2)


def solution(mesh):
    return jax.shard_map(
        body,
        mesh=mesh,
        in_specs=(
            P(("groups", "ctx"), "rep", "head"),
            P(("groups", "ctx"), "rep", "head"),
            P(("groups", "ctx"), "rep", "head"),
            P(("groups", "ctx"), "head"),
            P(("groups", "ctx"), "head"),
            P(("groups", "ctx"), "head", None),
        ),
        out_specs=P(("groups", "ctx"), "rep", "head"),
        check_vma=False,
    )
```
